256 devices in a mesh: row: 16 (over z_hi, x, core), col: 16 (over z_lo, y).
Axes of the slice: x: 4, y: 4, z: 8 (z_hi: 2, z_lo: 4; z = z_hi * 4 + z_lo), core: 2. Of those that a mesh axis runs over, the one named last changes fastest.
Arguments:
- features: bfloat16 [32768, 768], P(('row', 'col')), may hold values from -6 to 6
- self_weight: bfloat16 [768, 768], replicated, may hold values from -0.21875 to 0.21875
- rel_weight: bfloat16 [768, 5, 768], replicated, may hold values from -0.21875 to 0.21875
- bias: float32 [768], replicated, may hold values from -3 to 3
- blocks: bfloat16 [16, 16, 5, 8, 128, 128], P('row', 'col'), may hold values from -0.083496094 to 0.083496094
- block_rows: int32 [16, 16, 5, 8], P('row', 'col'), may hold values from 0 to 15
- block_cols: int32 [16, 16, 5, 8], P('row', 'col'), may hold values from 0 to 15
- block_counts: int32 [16, 16, 5], P('row', 'col'), may hold values from 1 to 8, as said below
Outputs:
- layer_out: bfloat16 [32768, 768], P(('row', 'col'))
The draws below stay inside these ranges and needn't reach their ends.
Inputs may be any that keep to these rules, and one draw needn't show every extreme that they name: The live slots of a tile and relation are its first block_counts slots; the others are ignored. `block_rows`: pairs of destination and source blocks may repeat within a tile.
All inputs are finite; a program needn't handle non-finite values.
Results may differ from the reference program's by a relative error of at most 0.014.
Values may be sent and summed in bfloat16 or wider, within the bound.
No kernel may reach another device: no remote copies, remote signals or barrier semaphores. Data moves between devices by JAX's collectives and lax.ppermute only.
A program may use at most 128 MiB of HBM per device.

```python
import jax
import jax.numpy as jnp
from jax import lax

D = 768
REL = 5
BLOCK = 128
ROWS_DEV = 128
SLOTS = 8
NODES = 32768
BROWS = 16
BCOLS = 16
N_ROW = 16
N_COL = 16


def draw_block_counts(key, part):
    first_key, second_key = jax.random.split(jax.random.fold_in(key, 17))
    total = N_ROW * N_COL * REL
    spread = jax.random.randint(first_key, (total,), 0, SLOTS)
    counts = 1 + spread * spread // SLOTS
    chosen = jax.random.randint(second_key, (), 0, total)
    counts = jnp.where(jnp.arange(total) == chosen, SLOTS, counts)
    return counts.reshape(N_ROW, N_COL, REL).astype(jnp.int32)


def plant(drawn, rng, smallest, largest):
    index_at = [jax.random.randint(jax.random.fold_in(rng, axis), (), 0, length) for axis, length in enumerate(drawn.shape)]
    main_axis = drawn.shape.index(max(drawn.shape))
    neighbour = index_at[:main_axis] + [(index_at[main_axis] + 1) % drawn.shape[main_axis]] + index_at[main_axis + 1:]
    return drawn.at[tuple(index_at)].set(smallest).at[tuple(neighbour)].set(largest)


def level_of(rng, extent, cuts, least, high):
    loudness = 1.0
    for dim, blocks in cuts:
        heights = jax.random.uniform(jax.random.fold_in(jax.random.fold_in(rng, 6), dim), (blocks,), jnp.float32, least / len(cuts), high / len(cuts))
        loudness = loudness * jnp.repeat(jnp.exp(heights), extent[dim] // blocks).reshape((-1,) + (1,) * (len(extent) - 1 - dim))
    return loudness


def bell_draw(stream_key, dims, deviation, most, cuts=(), kind=jnp.bfloat16):
    result = jax.random.normal(stream_key, dims, jnp.float32) * deviation
    if len(cuts) > 0:
        result = level_of(stream_key, dims, cuts, -0.22, 0.18) * result
    return jnp.clip(result, min=-most, max=most).astype(kind)


def setup_inputs(seed: int = 0) -> dict:
    arg_keys = jax.random.split(jax.random.key(seed), 9)
    features = bell_draw(arg_keys[0], (NODES, D), 1.0, 6.0, ((0, 256),))
    self_weight = bell_draw(arg_keys[1], (D, D), D ** -0.5, 0.21875)
    rel_weight = bell_draw(arg_keys[2], (D, REL, D), D ** -0.5, 0.21875)
    bias = bell_draw(arg_keys[3], (D,), 0.5, 3.0, (), jnp.float32)
    blocks = bell_draw(arg_keys[4], (N_ROW, N_COL, REL, SLOTS, BLOCK, BLOCK), ((ROWS_DEV / (SLOTS * REL)) ** 0.5 / BLOCK), 0.083496094, ((0, 16), (1, 16)))
    block_rows = plant(jax.random.randint(arg_keys[5], (N_ROW, N_COL, REL, SLOTS), 0, BROWS), jax.random.fold_in(arg_keys[5], 1), 0, BROWS - 1).astype(jnp.int32)
    block_cols = plant(jax.random.randint(arg_keys[6], (N_ROW, N_COL, REL, SLOTS), 0, BCOLS), jax.random.fold_in(arg_keys[6], 1), 0, BCOLS - 1).astype(jnp.int32)
    block_counts = draw_block_counts(jax.random.fold_in(arg_keys[8], 71), 0)
    return {"features": features, "self_weight": self_weight, "rel_weight": rel_weight, "bias": bias, "blocks": blocks, "block_rows": block_rows, "block_cols": block_cols, "block_counts": block_counts}


def tile_sum(tile_blocks, tile_rows, tile_cols, tile_counts, panel):
    slots = tile_blocks.shape[1]
    width = panel.shape[-1]
    total = jnp.zeros((BROWS, BLOCK, width), jnp.float32)
    for relation in range(REL):
        source = panel[:, :, relation, :]
        chosen = source[tile_cols[relation]]
        live = (jnp.arange(slots, dtype=jnp.int32) < tile_counts[relation]).astype(jnp.float32)
        owners = (tile_rows[relation][None, :] == jnp.arange(BROWS, dtype=jnp.int32)[:, None]).astype(jnp.float32) * live[None, :]
        products = jnp.einsum("sik,skd->sid", tile_blocks[relation].astype(jnp.float32), chosen.astype(jnp.float32))
        total = total + jnp.einsum("ns,sid->nid", owners, products, precision=lax.Precision.HIGHEST)
    rounded = lax.optimization_barrier(total.astype(jnp.bfloat16))
    return rounded.astype(jnp.float32).reshape(BROWS * BLOCK, width)


def reference(features, self_weight, rel_weight, bias, blocks, block_rows, block_cols, block_counts):
    nodes, width = features.shape
    stacked = rel_weight.reshape(width, REL * width)
    transformed = jnp.dot(features, stacked, preferred_element_type=jnp.float32).astype(jnp.bfloat16)
    grouped = transformed.reshape(N_ROW, N_COL, ROWS_DEV, REL, width)

    def row_group(inputs):
        group_blocks, group_rows, group_cols, group_counts = inputs

        def step(total, item):
            column, one_blocks, one_rows, one_cols, one_counts = item
            panel = lax.dynamic_index_in_dim(grouped, column, axis=1, keepdims=False)
            panel = panel.reshape(BCOLS, BLOCK, REL, width)
            return total + tile_sum(one_blocks, one_rows, one_cols, one_counts, panel), None

        init = jnp.zeros((BROWS * BLOCK, width), jnp.float32)
        columns = jnp.arange(N_COL, dtype=jnp.int32)
        total, _ = lax.scan(step, init, (columns, group_blocks, group_rows, group_cols, group_counts))
        return total

    aggregate = lax.map(row_group, (blocks, block_rows, block_cols, block_counts))
    aggregate = aggregate.reshape(nodes, width)
    self_term = jnp.dot(features, self_weight, preferred_element_type=jnp.float32)
    return jnp.maximum(self_term + aggregate + bias, 0.0).astype(jnp.bfloat16)
```

```python
import functools

import jax
import jax.numpy as jnp
from jax import lax
from jax.experimental import pallas as pl
from jax.experimental.pallas import tpu as pltpu
from jax.sharding import PartitionSpec as P


def tile_kernel(
    slots, rows_ref, cols_ref, counts_ref, blocks_ref, panel_ref, weight_ref, out_ref, total, picked
):
    relations = weight_ref.shape[0]
    size = blocks_ref.shape[-1]
    total[...] = jnp.zeros_like(total)
    for relation in range(relations):
        live = counts_ref[relation]

        def pick(slot, carry):
            at = relation * slots + slot
            source = pl.multiple_of(cols_ref[at] * size, size)
            product = jnp.dot(
                blocks_ref[at], panel_ref[pl.ds(source, size), :], preferred_element_type=jnp.float32
            )
            picked[pl.ds(pl.multiple_of(slot * size, size), size), :] = product.astype(picked.dtype)
            return carry

        lax.fori_loop(0, live, pick, 0)

        def spread(pair, carry):
            first = pl.multiple_of(pair * 2 * size, 2 * size)
            moved = jnp.dot(
                picked[pl.ds(first, 2 * size), :],
                weight_ref[relation],
                preferred_element_type=jnp.float32,
            )
            for half in range(2):
                slot = pair * 2 + half

                @pl.when(slot < live)
                def _():
                    target = pl.multiple_of(rows_ref[relation * slots + slot] * size, size)
                    total[pl.ds(target, size), :] += moved[half * size : (half + 1) * size]

            return carry

        lax.fori_loop(0, (live + 1) // 2, spread, 0)
    out_ref[...] = total[...].astype(out_ref.dtype)


def aggregate_tile(tile_blocks, tile_rows, tile_cols, tile_counts, panel, weights, brows):
    relations, slots, size, _ = tile_blocks.shape
    width = panel.shape[-1]
    vmem = pl.BlockSpec(memory_space=pltpu.VMEM)
    smem = pl.BlockSpec(memory_space=pltpu.SMEM)
    return pl.pallas_call(
        functools.partial(tile_kernel, slots),
        out_shape=jax.ShapeDtypeStruct((brows * size, width), jnp.bfloat16),
        in_specs=[smem, smem, smem, vmem, vmem, vmem],
        out_specs=vmem,
        scratch_shapes=[
            pltpu.VMEM((brows * size, width), jnp.float32),
            pltpu.VMEM((slots * size, width), jnp.bfloat16),
        ],
        compiler_params=pltpu.CompilerParams(vmem_limit_bytes=32 << 20),
        name="tile",
    )(
        tile_rows.reshape(-1),
        tile_cols.reshape(-1),
        tile_counts,
        tile_blocks.reshape(relations * slots, size, size),
        panel,
        weights,
    )


def per_device(
    features, self_weight, rel_weight, bias, blocks, block_rows, block_cols, block_counts
):
    rows_dev, width = features.shape
    size = blocks.shape[-1]
    brows = rows_dev * lax.axis_size("col") // size
    weights = jnp.transpose(rel_weight, (1, 0, 2))
    panel = lax.all_gather(features, "row", axis=0, tiled=True)
    partial_rows = aggregate_tile(
        blocks[0, 0], block_rows[0, 0], block_cols[0, 0], block_counts[0, 0], panel, weights, brows
    )
    owned_sum = lax.psum_scatter(partial_rows, "col", scatter_dimension=0, tiled=True)
    self_term = jnp.dot(features, self_weight, preferred_element_type=jnp.float32)
    return jnp.maximum(self_term + owned_sum.astype(jnp.float32) + bias, 0.0).astype(jnp.bfloat16)


def solution(mesh):
    return jax.shard_map(
        per_device,
        mesh=mesh,
        in_specs=(
            P(("row", "col"), None),
            P(),
            P(),
            P(),
            P("row", "col", None, None, None, None),
            P("row", "col", None, None),
            P("row", "col", None, None),
            P("row", "col", None),
        ),
        out_specs=P(("row", "col"), None),
        check_vma=False,
    )
```

```python
import functools

import jax
import jax.numpy as jnp
from jax import lax
from jax.experimental import pallas as pl
from jax.experimental.pallas import tpu as pltpu
from jax.sharding import PartitionSpec as P

X, CORES, Z, Y = 4, 2, 4, 4
SPLIT = 512


def row_shift(value, dz, dx, dc):
    pairs = []
    for index in range(16):
        z, x, c = index // 8, index // 2 % 4, index % 2
        pairs.append((index, (z ^ dz) * 8 + (x + dx) % X * 2 + (c ^ dc)))
    return lax.ppermute(value, "row", pairs)


def col_shift(value, dz, dy):
    pairs = []
    for index in range(16):
        z, y = index // 4, index % 4
        pairs.append((index, (z + dz) % Z * 4 + (y + dy) % Y))
    return lax.ppermute(value, "col", pairs)


def tile_kernel(
    slots, rows_ref, cols_ref, counts_ref, blocks_ref, weight_ref, *rest
):
    group_refs, y_refs, z_refs, (total, picked) = rest[:4], rest[4:8], rest[8:12], rest[12:]
    relations = weight_ref.shape[0]
    size = blocks_ref.shape[-1]
    total[...] = jnp.zeros_like(total)
    for relation in range(relations):
        live = counts_ref[relation]

        def pick(slot, carry):
            at = relation * slots + slot
            place = cols_ref[at]
            source = pl.multiple_of(place % 4 * size, size)
            out_rows = pl.ds(pl.multiple_of(slot * size, size), size)
            for group, group_ref in enumerate(group_refs):

                @pl.when(place // 4 == group)
                def _():
                    product = jnp.dot(
                        blocks_ref[at],
                        group_ref[pl.ds(source, size), :],
                        preferred_element_type=jnp.float32,
                    )
                    picked[out_rows, :] = product.astype(picked.dtype)

            return carry

        lax.fori_loop(0, live, pick, 0)

        def spread(pair, carry):
            first = pl.multiple_of(pair * 2 * size, 2 * size)
            moved = jnp.dot(
                picked[pl.ds(first, 2 * size), :],
                weight_ref[relation],
                preferred_element_type=jnp.float32,
            )
            for half in range(2):
                slot = pair * 2 + half

                @pl.when(slot < live)
                def _():
                    target = pl.multiple_of(rows_ref[relation * slots + slot] * size, size)
                    total[pl.ds(target, size), :] += moved[half * size : (half + 1) * size]

            return carry

        lax.fori_loop(0, (live + 1) // 2, spread, 0)
    for d in range(Y):
        for e in range(Z):
            rows = pl.ds((d * Z + e) * size, size)
            y_refs[d][e] = total[rows, :SPLIT].astype(jnp.bfloat16)
            z_refs[e][d] = total[rows, SPLIT:].astype(jnp.bfloat16)


def merge_kernel(own_ref, *refs):
    ins, (keep_ref, *send_refs) = refs[:3], refs[3:]
    for e in range(len(send_refs) + 1):
        summed = own_ref[e].astype(jnp.float32)
        for ref in ins:
            summed += ref[e].astype(jnp.float32)
        if e == 0:
            keep_ref[...] = summed
        else:
            send_refs[e - 1][...] = summed.astype(jnp.bfloat16)


def merge(own, ins):
    vmem = pl.BlockSpec(memory_space=pltpu.VMEM)
    count, rows, columns = own.shape
    return pl.pallas_call(
        merge_kernel,
        out_shape=[jax.ShapeDtypeStruct((rows, columns), jnp.float32)]
        + [jax.ShapeDtypeStruct((rows, columns), jnp.bfloat16)] * (count - 1),
        in_specs=[vmem] * 4,
        out_specs=[vmem] * count,
        compiler_params=pltpu.CompilerParams(vmem_limit_bytes=4 << 20),
        name="merge",
    )(own, *ins)


def aggregate_tile(tile_blocks, tile_rows, tile_cols, tile_counts, groups, weights):
    relations, slots, size, _ = tile_blocks.shape
    width = weights.shape[-1]
    vmem = pl.BlockSpec(memory_space=pltpu.VMEM)
    smem = pl.BlockSpec(memory_space=pltpu.SMEM)
    y_shape = jax.ShapeDtypeStruct((Z, size, SPLIT), jnp.bfloat16)
    z_shape = jax.ShapeDtypeStruct((Y, size, width - SPLIT), jnp.bfloat16)
    outs = pl.pallas_call(
        functools.partial(tile_kernel, slots),
        out_shape=[y_shape] * Y + [z_shape] * Z,
        in_specs=[smem] * 3 + [vmem] * 6,
        out_specs=[vmem] * (Y + Z),
        scratch_shapes=[
            pltpu.VMEM((Y * Z * size, width), jnp.float32),
            pltpu.VMEM((slots * size, width), jnp.bfloat16),
        ],
        compiler_params=pltpu.CompilerParams(vmem_limit_bytes=32 << 20),
        name="tile",
    )(
        tile_rows.reshape(-1),
        tile_cols.reshape(-1),
        tile_counts,
        tile_blocks.reshape(relations * slots, size, size),
        weights,
        *groups,
    )
    return outs[:Y], outs[Y:]


def gather_groups(features, self_term):
    far = row_shift(features, 1, 0, 0)
    near_parts = [features] + [row_shift(features, 0, d, 0) for d in (1, 3, 2)]
    far, self_term = lax.optimization_barrier((far, self_term))
    far_parts = [far] + [row_shift(far, 0, d, 0) for d in (1, 3, 2)]
    near = jnp.concatenate(near_parts, axis=0)
    near_other = row_shift(near, 0, 0, 1)
    rest = jnp.concatenate(far_parts, axis=0)
    rest_other = row_shift(rest, 0, 0, 1)
    return (near, rest, near_other, rest_other), self_term


def panel_place(source, me):
    z, x, c = source // 8 ^ me // 8, (me // 2 - source // 2) % X, source % 2 ^ me % 2
    place = jnp.where(x == 2, 3, jnp.where(x == 3, 2, x))
    return c * 8 + z * 4 + place


def scatter_sum(y_parts, z_parts):
    y_in = [col_shift(y_parts[d], 0, d) for d in (1, 3, 2)]
    z_in = [col_shift(z_parts[e], e, 0) for e in (1, 3, 2)]
    z_own, *z_send = merge(z_parts[0], z_in)
    y_own, *y_send = merge(y_parts[0], y_in)
    z_last = [col_shift(z_send[d - 1], 0, d) for d in (1, 3, 2)]
    y_last = [col_shift(y_send[e - 1], e, 0) for e in (1, 3, 2)]
    y_own += sum(part.astype(jnp.float32) for part in y_last)
    z_own += sum(part.astype(jnp.float32) for part in z_last)
    return y_own, z_own


def per_device(
    features, self_weight, rel_weight, bias, blocks, block_rows, block_cols, block_counts
):
    row_me, col_me = lax.axis_index("row"), lax.axis_index("col")
    weights = jnp.transpose(rel_weight, (1, 0, 2))
    targets = (block_rows[0, 0] % Y - col_me % Y) % Y * Z + (block_rows[0, 0] // Y - col_me // Y) % Z
    sources = panel_place(block_cols[0, 0], row_me)
    self_term = jnp.dot(features, self_weight, preferred_element_type=jnp.float32) + bias
    groups, self_term = gather_groups(features, self_term)
    y_parts, z_parts = aggregate_tile(
        blocks[0, 0], targets, sources, block_counts[0, 0], groups, weights
    )
    y_own, z_own = scatter_sum(y_parts, z_parts)
    owned = jnp.concatenate([y_own, z_own], axis=1)
    return jnp.maximum(self_term + owned, 0.0).astype(jnp.bfloat16)


def solution(mesh):
    return jax.shard_map(
        per_device,
        mesh=mesh,
        in_specs=(
            P(("row", "col"), None),
            P(),
            P(),
            P(),
            P("row", "col", None, None, None, None),
            P("row", "col", None, None),
            P("row", "col", None, None),
            P("row", "col", None),
        ),
        out_specs=P(("row", "col"), None),
        check_vma=False,
    )
```

```python
import functools

import jax
import jax.numpy as jnp
from jax import lax
from jax.experimental import pallas as pl
from jax.experimental.pallas import tpu as pltpu
from jax.sharding import PartitionSpec as P

X, CORES, Z, Y = 4, 2, 4, 4
SPLIT = 512
UNROLL, QUAD = 4, 4


def row_shift(value, dz, dx, dc):
    pairs = []
    for index in range(16):
        z, x, c = index // 8, index // 2 % 4, index % 2
        pairs.append((index, (z ^ dz) * 8 + (x + dx) % X * 2 + (c ^ dc)))
    return lax.ppermute(value, "row", pairs)


def col_shift(value, dz, dy):
    pairs = []
    for index in range(16):
        z, y = index // 4, index % 4
        pairs.append((index, (z + dz) % Z * 4 + (y + dy) % Y))
    return lax.ppermute(value, "col", pairs)


def rows_at(index, size):
    return pl.ds(pl.multiple_of(index * size, size), size)


def stage_kernel(group, first, last, codes_ref, starts_ref, blocks_ref, weight_ref, group_ref, *refs):
    if not first:
        refs = refs[1:]
    total, refs = refs[0], refs[1:]
    if last:
        y_refs, z_refs, refs = refs[:Y], refs[Y : Y + Z], refs[Y + Z :]
    (picked,) = refs
    relations = weight_ref.shape[0]
    size = blocks_ref.shape[-1]
    if first:
        total[...] = jnp.zeros_like(total)
    base = starts_ref[group * relations]
    length = starts_ref[(group + 1) * relations] - base

    def pick(step, carry):
        for u in range(UNROLL):
            n = jnp.minimum(step * UNROLL + u, length - 1)
            code = codes_ref[base + n]
            product = jnp.dot(
                blocks_ref[code // 64],
                group_ref[rows_at(code // 16 % 4, size), :],
                preferred_element_type=jnp.float32,
            )
            picked[rows_at(n, size), :] = product.astype(picked.dtype)
        return carry

    lax.fori_loop(0, (length + UNROLL - 1) // UNROLL, pick, 0)

    def spread(relation, carry):
        start = starts_ref[group * relations + relation]
        end = starts_ref[group * relations + relation + 1]

        def quad(step, carry):
            begin = start + step * QUAD
            for count in range(1, QUAD + 1):
                enough = (end - begin >= count) if count == QUAD else (end - begin == count)

                @pl.when(enough)
                def _():
                    moved = jnp.dot(
                        picked[pl.ds(pl.multiple_of((begin - base) * size, size), count * size), :],
                        weight_ref[relation],
                        preferred_element_type=jnp.float32,
                    )
                    for part in range(count):
                        target = rows_at(codes_ref[begin + part] % 16, size)
                        total[target, :] += moved[part * size : (part + 1) * size]

            return carry

        return lax.fori_loop(0, (end - start + QUAD - 1) // QUAD, quad, carry)

    lax.fori_loop(0, relations, spread, 0)
    if last:
        for d in range(Y):
            for e in range(Z):
                rows = pl.ds((d * Z + e) * size, size)
                y_refs[d][e] = total[rows, :SPLIT].astype(jnp.bfloat16)
                z_refs[e][d] = total[rows, SPLIT:].astype(jnp.bfloat16)


def slot_tables(targets, sources, counts):
    relations, slots = targets.shape
    many = relations * slots
    at = jnp.arange(many, dtype=jnp.int32)
    target, source = targets.reshape(many), sources.reshape(many)
    live = at % slots < jnp.repeat(counts, slots)
    bin_of = jnp.where(live, source // 4 * relations + at // slots, 4 * relations)
    key = bin_of * many + at
    rank = jnp.sum((key[None, :] < key[:, None]).astype(jnp.int32), axis=1)
    code = at * 64 + source % 4 * 16 + target
    codes = jnp.sum(jnp.where(rank[None, :] == at[:, None], code[None, :], 0), axis=1)
    bins = jnp.arange(4 * relations + 1, dtype=jnp.int32)
    starts = jnp.sum((bin_of[None, :] < bins[:, None]).astype(jnp.int32), axis=1)
    return codes, starts


def tile_stage(group, tables, blocks, weights, value, total):
    relations, slots, size, _ = blocks.shape
    width = weights.shape[-1]
    first, last = group == 0, group == 3
    vmem = pl.BlockSpec(memory_space=pltpu.VMEM)
    smem = pl.BlockSpec(memory_space=pltpu.SMEM)
    out_shape = [jax.ShapeDtypeStruct((Y * Z * size, width), jnp.float32)]
    if last:
        out_shape += [jax.ShapeDtypeStruct((Z, size, SPLIT), jnp.bfloat16)] * Y
        out_shape += [jax.ShapeDtypeStruct((Y, size, width - SPLIT), jnp.bfloat16)] * Z
    args = [*tables, blocks.reshape(relations * slots, size, size), weights, value]
    if not first:
        args.append(total)
    return pl.pallas_call(
        functools.partial(stage_kernel, group, first, last),
        out_shape=out_shape,
        in_specs=[smem] * 2 + [vmem] * (len(args) - 2),
        out_specs=[vmem] * len(out_shape),
        scratch_shapes=[pltpu.VMEM((relations * slots * size, width), jnp.bfloat16)],
        input_output_aliases={} if first else {len(args) - 1: 0},
        compiler_params=pltpu.CompilerParams(vmem_limit_bytes=24 << 20),
        cost_estimate=pl.CostEstimate(flops=1 << 30, bytes_accessed=4 << 20, transcendentals=0),
        name="tile",
    )(*args)


def merge_kernel(own_ref, *refs):
    ins, (keep_ref, *send_refs) = refs[:3], refs[3:]
    for e in range(len(send_refs) + 1):
        summed = own_ref[e].astype(jnp.float32)
        for ref in ins:
            summed += ref[e].astype(jnp.float32)
        if e == 0:
            keep_ref[...] = summed
        else:
            send_refs[e - 1][...] = summed.astype(jnp.bfloat16)


def merge(own, ins):
    vmem = pl.BlockSpec(memory_space=pltpu.VMEM)
    count, rows, columns = own.shape
    return pl.pallas_call(
        merge_kernel,
        out_shape=[jax.ShapeDtypeStruct((rows, columns), jnp.float32)]
        + [jax.ShapeDtypeStruct((rows, columns), jnp.bfloat16)] * (count - 1),
        in_specs=[vmem] * 4,
        out_specs=[vmem] * count,
        compiler_params=pltpu.CompilerParams(vmem_limit_bytes=4 << 20),
        name="merge",
    )(own, *ins)


def gather_groups(features, self_term, stage):
    far = row_shift(features, 1, 0, 0)
    near_parts = [features] + [row_shift(features, 0, d, 0) for d in (1, 3, 2)]
    far, self_term = lax.optimization_barrier((far, self_term))
    far_parts = [far] + [row_shift(far, 0, d, 0) for d in (1, 3, 2)]
    near_parts[-1], far = lax.optimization_barrier((near_parts[-1], far))
    near = jnp.concatenate(near_parts, axis=0)
    near_other = row_shift(near, 0, 0, 1)
    (total,) = stage(0, near, None)
    (total,) = stage(1, near_other, total)
    far_parts[-1], total = lax.optimization_barrier((far_parts[-1], total))
    rest = jnp.concatenate(far_parts, axis=0)
    rest_other = row_shift(rest, 0, 0, 1)
    (total,) = stage(2, rest, total)
    _, *parts = stage(3, rest_other, total)
    return parts, self_term


def panel_place(source, me):
    z, x, c = source // 8 ^ me // 8, (me // 2 - source // 2) % X, source % 2 ^ me % 2
    place = jnp.where(x == 2, 3, jnp.where(x == 3, 2, x))
    return z * 8 + c * 4 + place


def scatter_sum(y_parts, z_parts):
    y_in = [col_shift(y_parts[d], 0, d) for d in (1, 3, 2)]
    z_in = [col_shift(z_parts[e], e, 0) for e in (1, 3, 2)]
    z_own, *z_send = merge(z_parts[0], z_in)
    y_own, *y_send = merge(y_parts[0], y_in)
    z_last = [col_shift(z_send[d - 1], 0, d) for d in (1, 3, 2)]
    y_last = [col_shift(y_send[e - 1], e, 0) for e in (1, 3, 2)]
    y_own += sum(part.astype(jnp.float32) for part in y_last)
    z_own += sum(part.astype(jnp.float32) for part in z_last)
    return y_own, z_own


def per_device(
    features, self_weight, rel_weight, bias, blocks, block_rows, block_cols, block_counts
):
    row_me, col_me = lax.axis_index("row"), lax.axis_index("col")
    weights = jnp.transpose(rel_weight, (1, 0, 2))
    targets = (block_rows[0, 0] % Y - col_me % Y) % Y * Z + (block_rows[0, 0] // Y - col_me // Y) % Z
    sources = panel_place(block_cols[0, 0], row_me)
    self_term = jnp.dot(features, self_weight, preferred_element_type=jnp.float32) + bias
    tables = slot_tables(targets, sources, block_counts[0, 0])
    stage = lambda index, value, total: tile_stage(index, tables, blocks[0, 0], weights, value, total)
    parts, self_term = gather_groups(features, self_term, stage)
    y_parts, z_parts = parts[:Y], parts[Y:]
    y_own, z_own = scatter_sum(y_parts, z_parts)
    owned = jnp.concatenate([y_own, z_own], axis=1)
    return jnp.maximum(self_term + owned, 0.0).astype(jnp.bfloat16)


def solution(mesh):
    return jax.shard_map(
        per_device,
        mesh=mesh,
        in_specs=(
            P(("row", "col"), None),
            P(),
            P(),
            P(),
            P("row", "col", None, None, None, None),
            P("row", "col", None, None),
            P("row", "col", None, None),
            P("row", "col", None),
        ),
        out_specs=P(("row", "col"), None),
        check_vma=False,
    )
```

```python
import functools

import jax
import jax.numpy as jnp
from jax import lax
from jax.experimental import pallas as pl
from jax.experimental.pallas import tpu as pltpu
from jax.sharding import PartitionSpec as P

X, CORES, Z, Y = 4, 2, 4, 4
SPLIT = 512
UNROLL, QUAD = 4, 4


def row_shift(value, dz, dx, dc):
    pairs = []
    for index in range(16):
        z, x, c = index // 8, index // 2 % 4, index % 2
        pairs.append((index, (z ^ dz) * 8 + (x + dx) % X * 2 + (c ^ dc)))
    return lax.ppermute(value, "row", pairs)


def col_shift(value, dz, dy):
    pairs = []
    for index in range(16):
        z, y = index // 4, index % 4
        pairs.append((index, (z + dz) % Z * 4 + (y + dy) % Y))
    return lax.ppermute(value, "col", pairs)


def rows_at(index, size):
    return pl.ds(pl.multiple_of(index * size, size), size)


def stage_kernel(group, first, last, codes_ref, starts_ref, blocks_ref, weight_ref, group_ref, *refs):
    if not first:
        refs = refs[1:]
    total, refs = refs[0], refs[1:]
    if last:
        y_refs, z_refs, refs = refs[:Y], refs[Y : Y + Z], refs[Y + Z :]
    (picked,) = refs
    relations = weight_ref.shape[0]
    size = blocks_ref.shape[-1]
    if first:
        total[...] = jnp.zeros_like(total)
    base = starts_ref[group * relations]
    length = starts_ref[(group + 1) * relations] - base

    def pick(step, carry):
        for u in range(UNROLL):
            n = jnp.minimum(step * UNROLL + u, length - 1)
            code = codes_ref[base + n]
            product = jnp.dot(
                blocks_ref[code // 64],
                group_ref[rows_at(code // 16 % 4, size), :],
                preferred_element_type=jnp.float32,
            )
            picked[rows_at(n, size), :] = product.astype(picked.dtype)
        return carry

    lax.fori_loop(0, (length + UNROLL - 1) // UNROLL, pick, 0)

    def spread(relation, carry):
        start = starts_ref[group * relations + relation]
        end = starts_ref[group * relations + relation + 1]

        def quad(step, carry):
            begin = start + step * QUAD
            for count in range(1, QUAD + 1):
                enough = (end - begin >= count) if count == QUAD else (end - begin == count)

                @pl.when(enough)
                def _():
                    moved = jnp.dot(
                        picked[pl.ds(pl.multiple_of((begin - base) * size, size), count * size), :],
                        weight_ref[relation],
                        preferred_element_type=jnp.float32,
                    )
                    for part in range(count):
                        target = rows_at(codes_ref[begin + part] % 16, size)
                        total[target, :] += moved[part * size : (part + 1) * size]

            return carry

        return lax.fori_loop(0, (end - start + QUAD - 1) // QUAD, quad, carry)

    lax.fori_loop(0, relations, spread, 0)
    if last:
        for d in range(Y):
            for e in range(Z):
                rows = pl.ds((d * Z + e) * size, size)
                y_refs[d][e] = total[rows, :SPLIT].astype(jnp.bfloat16)
                z_refs[e][d] = total[rows, SPLIT:].astype(jnp.bfloat16)


def plan_kernel(
    slots, me_ref, rows_ref, cols_ref, counts_ref, codes_ref, starts_ref
):
    relations = counts_ref.shape[2]
    row_me, col_me = me_ref[0], me_ref[1]

    def place_of(relation, slot):
        source = cols_ref[0, 0, relation, slot]
        z, c = (source // 8) ^ (row_me // 8), (source % 2) ^ (row_me % 2)
        return z * 2 + c, source // 2 % X

    for index in range(4 * relations + 1):
        starts_ref[index] = 0
    for relation in range(relations):

        def count(slot, carry):
            group, _ = place_of(relation, slot)
            index = group * relations + relation + 1
            starts_ref[index] = starts_ref[index] + 1
            return carry

        lax.fori_loop(0, counts_ref[0, 0, relation], count, 0)
    for index in range(1, 4 * relations + 1):
        starts_ref[index] = starts_ref[index] + starts_ref[index - 1]
    for relation in range(relations):

        def put(slot, carry):
            group, place = place_of(relation, slot)
            target = rows_ref[0, 0, relation, slot]
            y = (target % Y - col_me % Y + Y) % Y
            z = (target // Y - col_me // Y + Z) % Z
            index = group * relations + relation
            at = starts_ref[index]
            codes_ref[at] = (relation * slots + slot) * 64 + place * 16 + y * Z + z
            starts_ref[index] = at + 1
            return carry

        lax.fori_loop(0, counts_ref[0, 0, relation], put, 0)
    for index in range(4 * relations - 1, 0, -1):
        starts_ref[index] = starts_ref[index - 1]
    starts_ref[0] = 0


def plan(me, block_rows, block_cols, block_counts):
    relations, slots = block_rows.shape[2:]
    smem = pl.BlockSpec(memory_space=pltpu.SMEM)
    many = relations * slots
    return pl.pallas_call(
        functools.partial(plan_kernel, slots),
        out_shape=[
            jax.ShapeDtypeStruct((many,), jnp.int32),
            jax.ShapeDtypeStruct((4 * relations + 1,), jnp.int32),
        ],
        in_specs=[smem] * 4,
        out_specs=[smem] * 2,
        compiler_params=pltpu.CompilerParams(vmem_limit_bytes=1 << 20),
        name="plan",
    )(me, block_rows, block_cols, block_counts)


def tile_stage(group, tables, blocks, weights, value, total):
    many, size, _ = blocks.shape
    width = weights.shape[-1]
    first, last = group == 0, group == 3
    vmem = pl.BlockSpec(memory_space=pltpu.VMEM)
    smem = pl.BlockSpec(memory_space=pltpu.SMEM)
    out_shape = [jax.ShapeDtypeStruct((Y * Z * size, width), jnp.float32)]
    if last:
        out_shape += [jax.ShapeDtypeStruct((Z, size, SPLIT), jnp.bfloat16)] * Y
        out_shape += [jax.ShapeDtypeStruct((Y, size, width - SPLIT), jnp.bfloat16)] * Z
    args = [*tables, blocks, weights, value]
    if not first:
        args.append(total)
    return pl.pallas_call(
        functools.partial(stage_kernel, group, first, last),
        out_shape=out_shape,
        in_specs=[smem] * 2 + [vmem] * (len(args) - 2),
        out_specs=[vmem] * len(out_shape),
        scratch_shapes=[pltpu.VMEM((many * size, width), jnp.bfloat16)],
        input_output_aliases={} if first else {len(args) - 1: 0},
        compiler_params=pltpu.CompilerParams(vmem_limit_bytes=24 << 20),
        cost_estimate=pl.CostEstimate(flops=1 << 30, bytes_accessed=4 << 20, transcendentals=0),
        name="tile",
    )(*args)


def merge_kernel(own_ref, *refs):
    ins, (keep_ref, *send_refs) = refs[:3], refs[3:]
    for e in range(len(send_refs) + 1):
        summed = own_ref[e].astype(jnp.float32)
        for ref in ins:
            summed += ref[e].astype(jnp.float32)
        if e == 0:
            keep_ref[...] = summed
        else:
            send_refs[e - 1][...] = summed.astype(jnp.bfloat16)


def merge(own, ins):
    vmem = pl.BlockSpec(memory_space=pltpu.VMEM)
    count, rows, columns = own.shape
    return pl.pallas_call(
        merge_kernel,
        out_shape=[jax.ShapeDtypeStruct((rows, columns), jnp.float32)]
        + [jax.ShapeDtypeStruct((rows, columns), jnp.bfloat16)] * (count - 1),
        in_specs=[vmem] * 4,
        out_specs=[vmem] * count,
        compiler_params=pltpu.CompilerParams(vmem_limit_bytes=4 << 20),
        name="merge",
    )(own, *ins)


X_GROUPS = [[z * 8 + x * 2 + c for x in range(X)] for z in range(2) for c in range(CORES)]
Y_GROUPS = [[z * Y + y for y in range(Y)] for z in range(Z)]
Z_GROUPS = [[z * Y + y for z in range(Z)] for y in range(Y)]


def along_x(value):
    copies = jnp.broadcast_to(value[None], (X, *value.shape))
    got = lax.all_to_all(copies, "row", 0, 0, axis_index_groups=X_GROUPS)
    return got.reshape(X * value.shape[0], value.shape[1])


def gather_groups(features, self_weight, tables, blocks, weights):
    stage = lambda index, value, total, tables: tile_stage(index, tables, blocks, weights, value, total)
    far = row_shift(features, 1, 0, 0)
    near = along_x(features)
    self_term = jnp.dot(features, self_weight, preferred_element_type=jnp.float32)
    far, self_term, tables = lax.optimization_barrier((far, self_term, tables))
    rest = along_x(far)
    near_other = row_shift(near, 0, 0, 1)
    (total,) = stage(0, near, None, tables)
    (total,) = stage(1, near_other, total, tables)
    rest, total = lax.optimization_barrier((rest, total))
    rest_other = row_shift(rest, 0, 0, 1)
    (total,) = stage(2, rest, total, tables)
    return self_term, stage(3, rest_other, total, tables)[1:]


def scatter_sum(y_parts, z_parts):
    y_in = [col_shift(y_parts[d], 0, d) for d in (1, 3, 2)]
    z_in = [col_shift(z_parts[e], e, 0) for e in (1, 3, 2)]
    y_own, *y_send = merge(y_parts[0], y_in)
    z_in, y_send = lax.optimization_barrier((z_in, y_send))
    z_own, *z_send = merge(z_parts[0], z_in)
    z_last = [col_shift(z_send[d - 1], 0, d) for d in (1, 3, 2)]
    y_last = [col_shift(y_send[e - 1], e, 0) for e in (1, 3, 2)]
    y_own += sum(part.astype(jnp.float32) for part in y_last)
    y_own, z_last = lax.optimization_barrier((y_own, z_last))
    z_own += sum(part.astype(jnp.float32) for part in z_last)
    return y_own, z_own


def per_device(
    features, self_weight, rel_weight, bias, blocks, block_rows, block_cols, block_counts
):
    relations, slots, size, _ = blocks.shape[2:]
    me = jnp.stack([lax.axis_index("row"), lax.axis_index("col")])
    weights = jnp.transpose(rel_weight, (1, 0, 2))
    blocks = blocks.reshape(relations * slots, size, size)
    tables = plan(me, block_rows, block_cols, block_counts)
    self_term, parts = gather_groups(features, self_weight, tables, blocks, weights)
    y_parts, z_parts = parts[:Y], parts[Y:]
    y_own, z_own = scatter_sum(y_parts, z_parts)
    owned = jnp.concatenate([y_own, z_own], axis=1)
    return jnp.maximum(self_term + owned + bias, 0.0).astype(jnp.bfloat16)


def solution(mesh):
    return jax.shard_map(
        per_device,
        mesh=mesh,
        in_specs=(
            P(("row", "col"), None),
            P(),
            P(),
            P(),
            P("row", "col", None, None, None, None),
            P("row", "col", None, None),
            P("row", "col", None, None),
            P("row", "col", None),
        ),
        out_specs=P(("row", "col"), None),
        check_vma=False,
    )
```

```python
import functools

import jax
import jax.numpy as jnp
from jax import lax
from jax.experimental import pallas as pl
from jax.experimental.pallas import tpu as pltpu
from jax.sharding import PartitionSpec as P

X, CORES, Z, Y = 4, 2, 4, 4
SPLIT = 512
UNROLL, QUAD = 4, 4


def row_shift(value, dz, dx, dc):
    pairs = []
    for index in range(16):
        z, x, c = index // 8, index // 2 % 4, index % 2
        pairs.append((index, (z ^ dz) * 8 + (x + dx) % X * 2 + (c ^ dc)))
    return lax.ppermute(value, "row", pairs)


def col_shift(value, dz, dy):
    pairs = []
    for index in range(16):
        z, y = index // 4, index % 4
        pairs.append((index, (z + dz) % Z * 4 + (y + dy) % Y))
    return lax.ppermute(value, "col", pairs)


def rows_at(index, size):
    return pl.ds(pl.multiple_of(index * size, size), size)


def stage_kernel(group, first, last, codes_ref, starts_ref, blocks_ref, weight_ref, group_ref, *refs):
    if not first:
        refs = refs[1:]
    total, refs = refs[0], refs[1:]
    if last:
        y_refs, z_refs, refs = refs[:Y], refs[Y : Y + Z], refs[Y + Z :]
    (picked,) = refs
    relations = weight_ref.shape[0]
    size = blocks_ref.shape[-1]
    if first:
        total[...] = jnp.zeros_like(total)
    base = starts_ref[group * relations]
    length = starts_ref[(group + 1) * relations] - base

    def pick(step, carry):
        for u in range(UNROLL):
            n = jnp.minimum(step * UNROLL + u, length - 1)
            code = codes_ref[base + n]
            product = jnp.dot(
                blocks_ref[code // 64],
                group_ref[rows_at(code // 16 % 4, size), :],
                preferred_element_type=jnp.float32,
            )
            picked[rows_at(n, size), :] = product.astype(picked.dtype)
        return carry

    lax.fori_loop(0, (length + UNROLL - 1) // UNROLL, pick, 0)

    def spread(relation, carry):
        start = starts_ref[group * relations + relation]
        end = starts_ref[group * relations + relation + 1]

        def quad(step, carry):
            begin = start + step * QUAD
            for count in range(1, QUAD + 1):
                enough = (end - begin >= count) if count == QUAD else (end - begin == count)

                @pl.when(enough)
                def _():
                    moved = jnp.dot(
                        picked[pl.ds(pl.multiple_of((begin - base) * size, size), count * size), :],
                        weight_ref[relation],
                        preferred_element_type=jnp.float32,
                    )
                    for part in range(count):
                        target = rows_at(codes_ref[begin + part] % 16, size)
                        total[target, :] += moved[part * size : (part + 1) * size]

            return carry

        return lax.fori_loop(0, (end - start + QUAD - 1) // QUAD, quad, carry)

    lax.fori_loop(0, relations, spread, 0)
    if last:
        for d in range(Y):
            for e in range(Z):
                rows = pl.ds((d * Z + e) * size, size)
                y_refs[d][e] = total[rows, :SPLIT].astype(jnp.bfloat16)
                z_refs[e][d] = total[rows, SPLIT:].astype(jnp.bfloat16)


def plan_kernel(
    slots, me_ref, rows_ref, cols_ref, counts_ref, codes_ref, starts_ref
):
    relations = counts_ref.shape[2]
    row_me, col_me = me_ref[0], me_ref[1]

    def place_of(relation, slot):
        source = cols_ref[0, 0, relation, slot]
        z, c = (source // 8) ^ (row_me // 8), (source % 2) ^ (row_me % 2)
        x = (row_me // 2 - source // 2 + 2 * X) % X
        return c * 2 + z, jnp.where(x == 2, 3, jnp.where(x == 3, 2, x))

    for index in range(4 * relations + 1):
        starts_ref[index] = 0
    for relation in range(relations):

        def count(slot, carry):
            group, _ = place_of(relation, slot)
            index = group * relations + relation + 1
            starts_ref[index] = starts_ref[index] + 1
            return carry

        lax.fori_loop(0, counts_ref[0, 0, relation], count, 0)
    for index in range(1, 4 * relations + 1):
        starts_ref[index] = starts_ref[index] + starts_ref[index - 1]
    for relation in range(relations):

        def put(slot, carry):
            group, place = place_of(relation, slot)
            target = rows_ref[0, 0, relation, slot]
            y = (target % Y - col_me % Y + Y) % Y
            z = (target // Y - col_me // Y + Z) % Z
            index = group * relations + relation
            at = starts_ref[index]
            codes_ref[at] = (relation * slots + slot) * 64 + place * 16 + y * Z + z
            starts_ref[index] = at + 1
            return carry

        lax.fori_loop(0, counts_ref[0, 0, relation], put, 0)
    for index in range(4 * relations - 1, 0, -1):
        starts_ref[index] = starts_ref[index - 1]
    starts_ref[0] = 0


def plan(me, block_rows, block_cols, block_counts):
    relations, slots = block_rows.shape[2:]
    smem = pl.BlockSpec(memory_space=pltpu.SMEM)
    many = relations * slots
    return pl.pallas_call(
        functools.partial(plan_kernel, slots),
        out_shape=[
            jax.ShapeDtypeStruct((many,), jnp.int32),
            jax.ShapeDtypeStruct((4 * relations + 1,), jnp.int32),
        ],
        in_specs=[smem] * 4,
        out_specs=[smem] * 2,
        compiler_params=pltpu.CompilerParams(vmem_limit_bytes=1 << 20),
        name="plan",
    )(me, block_rows, block_cols, block_counts)


def tile_stage(group, tables, blocks, weights, value, total):
    many, size, _ = blocks.shape
    width = weights.shape[-1]
    first, last = group == 0, group == 3
    vmem = pl.BlockSpec(memory_space=pltpu.VMEM)
    smem = pl.BlockSpec(memory_space=pltpu.SMEM)
    out_shape = [jax.ShapeDtypeStruct((Y * Z * size, width), jnp.float32)]
    if last:
        out_shape += [jax.ShapeDtypeStruct((Z, size, SPLIT), jnp.bfloat16)] * Y
        out_shape += [jax.ShapeDtypeStruct((Y, size, width - SPLIT), jnp.bfloat16)] * Z
    args = [*tables, blocks, weights, value]
    if not first:
        args.append(total)
    return pl.pallas_call(
        functools.partial(stage_kernel, group, first, last),
        out_shape=out_shape,
        in_specs=[smem] * 2 + [vmem] * (len(args) - 2),
        out_specs=[vmem] * len(out_shape),
        scratch_shapes=[pltpu.VMEM((many * size, width), jnp.bfloat16)],
        input_output_aliases={} if first else {len(args) - 1: 0},
        compiler_params=pltpu.CompilerParams(vmem_limit_bytes=14 << 20),
        cost_estimate=pl.CostEstimate(flops=1 << 30, bytes_accessed=4 << 20, transcendentals=0),
        name="tile",
    )(*args)


def merge_kernel(own_ref, *refs):
    ins, (keep_ref, *send_refs) = refs[:3], refs[3:]
    for e in range(len(send_refs) + 1):
        summed = own_ref[e].astype(jnp.float32)
        for ref in ins:
            summed += ref[e].astype(jnp.float32)
        if e == 0:
            keep_ref[...] = summed
        else:
            send_refs[e - 1][...] = summed.astype(jnp.bfloat16)


def merge(own, ins):
    vmem = pl.BlockSpec(memory_space=pltpu.VMEM)
    count, rows, columns = own.shape
    return pl.pallas_call(
        merge_kernel,
        out_shape=[jax.ShapeDtypeStruct((rows, columns), jnp.float32)]
        + [jax.ShapeDtypeStruct((rows, columns), jnp.bfloat16)] * (count - 1),
        in_specs=[vmem] * 4,
        out_specs=[vmem] * count,
        compiler_params=pltpu.CompilerParams(vmem_limit_bytes=4 << 20),
        name="merge",
    )(own, *ins)


def gather_groups(features, self_weight, tables, blocks, weights):
    far = row_shift(features, 1, 0, 0)
    near_parts = [features] + [row_shift(features, 0, d, 0) for d in (1, 3, 2)]
    self_term = jnp.dot(features, self_weight, preferred_element_type=jnp.float32)
    far, self_term, tables = lax.optimization_barrier((far, self_term, tables))
    stage = lambda index, value, total: tile_stage(index, tables, blocks, weights, value, total)
    far_parts = [far] + [row_shift(far, 0, d, 0) for d in (1, 3, 2)]

    near = jnp.concatenate(near_parts, axis=0)
    near_other = row_shift(near, 0, 0, 1)
    (total,) = stage(0, near, None)
    far_parts[-1], total = lax.optimization_barrier((far_parts[-1], total))
    rest = jnp.concatenate(far_parts, axis=0)
    rest_other = row_shift(rest, 0, 0, 1)
    (total,) = stage(1, rest, total)
    (total,) = stage(2, near_other, total)
    return self_term, stage(3, rest_other, total)[1:]


def scatter_sum(y_parts, z_parts):
    y_in = [col_shift(y_parts[d], 0, d) for d in (1, 3, 2)]
    z_in = [col_shift(z_parts[e], e, 0) for e in (1, 3, 2)]
    y_own, *y_send = merge(y_parts[0], y_in)
    z_in, y_send = lax.optimization_barrier((z_in, y_send))
    z_own, *z_send = merge(z_parts[0], z_in)
    z_last = [col_shift(z_send[d - 1], 0, d) for d in (1, 3, 2)]
    y_last = [col_shift(y_send[e - 1], e, 0) for e in (1, 3, 2)]
    y_own += sum(part.astype(jnp.float32) for part in y_last)
    y_own, z_last = lax.optimization_barrier((y_own, z_last))
    z_own += sum(part.astype(jnp.float32) for part in z_last)
    return y_own, z_own


def per_device(
    features, self_weight, rel_weight, bias, blocks, block_rows, block_cols, block_counts
):
    relations, slots, size, _ = blocks.shape[2:]
    me = jnp.stack([lax.axis_index("row"), lax.axis_index("col")])
    weights = jnp.transpose(rel_weight, (1, 0, 2))
    blocks = blocks.reshape(relations * slots, size, size)
    tables = plan(me, block_rows, block_cols, block_counts)
    self_term, parts = gather_groups(features, self_weight, tables, blocks, weights)
    y_parts, z_parts = parts[:Y], parts[Y:]
    y_own, z_own = scatter_sum(y_parts, z_parts)
    owned = jnp.concatenate([y_own, z_own], axis=1)
    return jnp.maximum(self_term + owned + bias, 0.0).astype(jnp.bfloat16)


def solution(mesh):
    return jax.shard_map(
        per_device,
        mesh=mesh,
        in_specs=(
            P(("row", "col"), None),
            P(),
            P(),
            P(),
            P("row", "col", None, None, None, None),
            P("row", "col", None, None),
            P("row", "col", None, None),
            P("row", "col", None),
        ),
        out_specs=P(("row", "col"), None),
        check_vma=False,
    )
```

```python
import functools

import jax
import jax.numpy as jnp
from jax import lax
from jax.experimental import pallas as pl
from jax.experimental.pallas import tpu as pltpu
from jax.sharding import PartitionSpec as P

Z, Y = 4, 4
SPLIT = 512
UNROLL, QUAD = 4, 4


def row_swap(value, dz, dx, dc):
    return lax.ppermute(value, "row", [(at, at ^ (dz * 8 + dx * 2 + dc)) for at in range(16)])


def col_swap(value, dz, dy):
    return lax.ppermute(value, "col", [(at, at ^ (dz * Y + dy)) for at in range(16)])


def rows_at(index, size):
    return pl.ds(pl.multiple_of(index * size, size), size)


def stage_kernel(group, first, last, codes_ref, starts_ref, blocks_ref, weight_ref, group_ref, *refs):
    if not first:
        refs = refs[1:]
    total, refs = refs[0], refs[1:]
    if last:
        y_refs, z_refs, refs = refs[:Y], refs[Y : Y + 2], refs[Y + 2 :]
    (picked,) = refs
    relations = weight_ref.shape[0]
    size = blocks_ref.shape[-1]
    if first:
        total[...] = jnp.zeros_like(total)
    base = starts_ref[group * relations]
    length = starts_ref[(group + 1) * relations] - base

    def pick(step, carry):
        for u in range(UNROLL):
            n = jnp.minimum(step * UNROLL + u, length - 1)
            code = codes_ref[base + n]
            product = jnp.dot(
                blocks_ref[code // 64],
                group_ref[rows_at(code // 16 % 4, size), :],
                preferred_element_type=jnp.float32,
            )
            picked[rows_at(n, size), :] = product.astype(picked.dtype)
        return carry

    lax.fori_loop(0, (length + UNROLL - 1) // UNROLL, pick, 0)

    def spread(relation, carry):
        start = starts_ref[group * relations + relation]
        end = starts_ref[group * relations + relation + 1]

        def quad(step, carry):
            begin = start + step * QUAD
            for count in range(1, QUAD + 1):
                enough = (end - begin >= count) if count == QUAD else (end - begin == count)

                @pl.when(enough)
                def _():
                    moved = jnp.dot(
                        picked[pl.ds(pl.multiple_of((begin - base) * size, size), count * size), :],
                        weight_ref[relation],
                        preferred_element_type=jnp.float32,
                    )
                    for part in range(count):
                        target = rows_at(codes_ref[begin + part] % 16, size)
                        total[target, :] += moved[part * size : (part + 1) * size]

            return carry

        return lax.fori_loop(0, (end - start + QUAD - 1) // QUAD, quad, carry)

    lax.fori_loop(0, relations, spread, 0)
    if last:
        for d in range(Y):
            for e in range(Z):
                rows = pl.ds((d * Z + e) * size, size)
                y_refs[d][e] = total[rows, :SPLIT].astype(jnp.bfloat16)
                z_refs[e % 2][e // 2, d] = total[rows, SPLIT:].astype(jnp.bfloat16)


def plan_kernel(relations, me_ref, table_ref, codes_ref, starts_ref):
    slots = table_ref.shape[0] // relations
    row_me, col_me = me_ref[0] >> 4, me_ref[0] & 15
    for index in range(4 * relations + 1):
        starts_ref[index] = 0

    def parts(at):
        packed = table_ref[at]
        source = (packed >> 4 & 15) ^ row_me
        target = (packed & 15) ^ col_me
        return packed >> 8, (source & 1) * 2 + (source >> 3), source >> 1 & 3, (target & 3) * 4 + (target >> 2)

    def per_slot(act):
        for relation in range(relations):
            live = table_ref[relation * slots] >> 8

            def body(slot, carry):
                at = relation * slots + slot
                _, group, place, target = parts(at)
                act(group * relations + relation, at, place, target)
                return carry

            lax.fori_loop(0, live, body, 0)

    def count(index, at, place, target):
        starts_ref[index + 1] = starts_ref[index + 1] + 1

    def put(index, at, place, target):
        spot = starts_ref[index]
        codes_ref[spot] = at * 64 + place * 16 + target
        starts_ref[index] = spot + 1

    per_slot(count)
    for index in range(1, 4 * relations + 1):
        starts_ref[index] = starts_ref[index] + starts_ref[index - 1]
    per_slot(put)
    for index in range(4 * relations - 1, 0, -1):
        starts_ref[index] = starts_ref[index - 1]
    starts_ref[0] = 0


def plan(me, block_rows, block_cols, block_counts):
    relations, slots = block_rows.shape[2:]
    smem = pl.BlockSpec(memory_space=pltpu.SMEM)
    many = relations * slots
    table = (block_rows + block_cols * 16 + block_counts[..., None] * 256).reshape(many)
    return pl.pallas_call(
        functools.partial(plan_kernel, relations),
        out_shape=[
            jax.ShapeDtypeStruct((many,), jnp.int32),
            jax.ShapeDtypeStruct((4 * relations + 1,), jnp.int32),
        ],
        in_specs=[smem] * 2,
        out_specs=[smem] * 2,
        compiler_params=pltpu.CompilerParams(vmem_limit_bytes=1 << 20),
        name="plan",
    )(me, table)


def tile_stage(group, tables, blocks, weights, value, total):
    many, size, _ = blocks.shape
    width = weights.shape[-1]
    first, last = group == 0, group == 3
    vmem = pl.BlockSpec(memory_space=pltpu.VMEM)
    smem = pl.BlockSpec(memory_space=pltpu.SMEM)
    out_shape = [jax.ShapeDtypeStruct((Y * Z * size, width), jnp.float32)]
    if last:
        out_shape += [jax.ShapeDtypeStruct((Z, size, SPLIT), jnp.bfloat16)] * Y
        out_shape += [jax.ShapeDtypeStruct((Z // 2, Y, size, width - SPLIT), jnp.bfloat16)] * 2
    args = [*tables, blocks, weights, value]
    if not first:
        args.append(total)
    return pl.pallas_call(
        functools.partial(stage_kernel, group, first, last),
        out_shape=out_shape,
        in_specs=[smem] * 2 + [vmem] * (len(args) - 2),
        out_specs=[vmem] * len(out_shape),
        scratch_shapes=[pltpu.VMEM((many * size, width), jnp.bfloat16)],
        input_output_aliases={} if first else {len(args) - 1: 0},
        compiler_params=pltpu.CompilerParams(vmem_limit_bytes=14 << 20),
        cost_estimate=pl.CostEstimate(flops=1 << 30, bytes_accessed=4 << 20, transcendentals=0),
        name="tile",
    )(*args)


def small(function, out_shape, *args):
    def kernel(*refs):
        function(refs[: len(args)], refs[len(args) :])

    vmem = pl.BlockSpec(memory_space=pltpu.VMEM)
    return pl.pallas_call(
        kernel,
        out_shape=out_shape,
        in_specs=[vmem] * len(args),
        out_specs=[vmem] * len(out_shape),
        compiler_params=pltpu.CompilerParams(vmem_limit_bytes=4 << 20),
        name="merge",
    )(*args)


def merge_y(ins, outs):
    for e in range(Z):
        summed = sum(ref[e].astype(jnp.float32) for ref in ins)
        outs[e][...] = summed.astype(outs[e].dtype)


def merge_z_near(ins, outs):
    own, got = ins
    outs[0][...] = own[0].astype(jnp.float32) + got[0].astype(jnp.float32)
    outs[1][...] = (own[1].astype(jnp.float32) + got[1].astype(jnp.float32)).astype(jnp.bfloat16)


def merge_z_far(ins, outs):
    kept, got = ins
    for d in range(Y):
        summed = kept[d] + got[d].astype(jnp.float32)
        if d == 0 or d == 3:
            outs[d // 3][...] = summed
        else:
            outs[2][d - 1] = summed.astype(jnp.bfloat16)


def merge_z_last(ins, outs):
    here, across, got = ins
    outs[0][...] = here[...] + got[0].astype(jnp.float32)
    outs[1][...] = (across[...] + got[1].astype(jnp.float32)).astype(jnp.bfloat16)


def gather_groups(features, self_weight, to_plan, blocks, weights):
    far = row_swap(features, 1, 0, 0)
    near_parts = [features] + [row_swap(features, 0, d, 0) for d in (1, 2, 3)]
    self_term = jnp.dot(features, self_weight, preferred_element_type=jnp.float32)
    far, self_term, to_plan = lax.optimization_barrier((far, self_term, to_plan))
    tables = plan(*to_plan)
    stage = lambda index, value, total: tile_stage(index, tables, blocks, weights, value, total)
    far_parts = [far] + [row_swap(far, 0, d, 0) for d in (1, 2, 3)]
    near = jnp.concatenate(near_parts, axis=0)
    near_other = row_swap(near, 0, 0, 1)
    (total,) = stage(0, near, None)
    far_parts[-1], total = lax.optimization_barrier((far_parts[-1], total))
    rest = jnp.concatenate(far_parts, axis=0)
    rest_other = row_swap(rest, 0, 0, 1)
    (total,) = stage(1, rest, total)
    (total,) = stage(2, near_other, total)
    return self_term, stage(3, rest_other, total)[1:]


def scatter_sum(parts):
    y_parts, (z_here, z_there) = parts[:Y], parts[Y:]
    f32, bf16 = jnp.float32, jnp.bfloat16
    many, size, columns = z_here.shape[1:]
    piece = (size, columns)
    z_near = col_swap(z_there, 1, 0)
    y_in = [col_swap(y_parts[d], 0, d) for d in (2, 1, 3)]
    shapes = [jax.ShapeDtypeStruct((many, *piece), f32), jax.ShapeDtypeStruct((many, *piece), bf16)]
    z_kept, z_send = small(merge_z_near, shapes, z_here, z_near)
    z_far = col_swap(z_send, 2, 0)
    shapes = [jax.ShapeDtypeStruct(piece, f32)] * 2 + [jax.ShapeDtypeStruct((2, *piece), bf16)]
    z_own, z_across, z_send = small(merge_z_far, shapes, z_kept, z_far)
    z_got = col_swap(z_send, 0, 1)
    y_in, z_across = lax.optimization_barrier((y_in, z_across))
    piece_y = y_parts[0].shape[1:]
    shapes = [jax.ShapeDtypeStruct(piece_y, f32)] + [jax.ShapeDtypeStruct(piece_y, bf16)] * 3
    y_own, *y_send = small(merge_y, shapes, y_parts[0], *y_in)
    y_last = [col_swap(y_send[e - 1], e, 0) for e in (2, 3, 1)]
    shapes = [jax.ShapeDtypeStruct(piece, f32), jax.ShapeDtypeStruct(piece, bf16)]
    z_own, z_send = small(merge_z_last, shapes, z_own, z_across, z_got)
    z_own += col_swap(z_send, 0, 3).astype(f32)
    y_last, z_own = lax.optimization_barrier((y_last, z_own))
    y_own += sum(part.astype(f32) for part in y_last)
    return y_own, z_own


def per_device(
    features, self_weight, rel_weight, bias, blocks, block_rows, block_cols, block_counts
):
    relations, slots, size, _ = blocks.shape[2:]
    me = (lax.axis_index("row") * 16 + lax.axis_index("col")).reshape(1)
    weights = jnp.transpose(rel_weight, (1, 0, 2))
    blocks = blocks.reshape(relations * slots, size, size)
    to_plan = (me, block_rows, block_cols, block_counts)
    self_term, parts = gather_groups(features, self_weight, to_plan, blocks, weights)
    y_own, z_own = scatter_sum(parts)
    owned = jnp.concatenate([y_own, z_own], axis=1)
    return jnp.maximum(self_term + owned + bias, 0.0).astype(jnp.bfloat16)


def solution(mesh):
    return jax.shard_map(
        per_device,
        mesh=mesh,
        in_specs=(
            P(("row", "col"), None),
            P(),
            P(),
            P(),
            P("row", "col", None, None, None, None),
            P("row", "col", None, None),
            P("row", "col", None, None),
            P("row", "col", None),
        ),
        out_specs=P(("row", "col"), None),
        check_vma=False,
    )
```

```python
import functools

import jax
import jax.numpy as jnp
from jax import lax
from jax.experimental import pallas as pl
from jax.experimental.pallas import tpu as pltpu
from jax.sharding import PartitionSpec as P

Z, Y = 4, 4
SPLIT = 512
UNROLL, QUAD = 4, 4


def row_swap(value, dz, dx, dc):
    return lax.ppermute(value, "row", [(at, at ^ (dz * 8 + dx * 2 + dc)) for at in range(16)])


def col_swap(value, dz, dy):
    return lax.ppermute(value, "col", [(at, at ^ (dz * Y + dy)) for at in range(16)])


def rows_at(index, size):
    return pl.ds(pl.multiple_of(index * size, size), size)


def stage_kernel(group, first, last, codes_ref, starts_ref, blocks_ref, weight_ref, group_ref, *refs):
    if not first:
        refs = refs[1:]
    total, refs = refs[0], refs[1:]
    if last:
        y_refs, z_refs, refs = refs[:Y], refs[Y : Y + 2], refs[Y + 2 :]
    (picked,) = refs
    relations = weight_ref.shape[0]
    size = blocks_ref.shape[-1]
    if first:
        total[...] = jnp.zeros_like(total)
    base = starts_ref[group * relations]
    length = starts_ref[(group + 1) * relations] - base

    def pick(step, carry):
        for u in range(UNROLL):
            n = jnp.minimum(step * UNROLL + u, length - 1)
            code = codes_ref[base + n]
            product = jnp.dot(
                blocks_ref[code // 64],
                group_ref[rows_at(code // 16 % 4, size), :],
                preferred_element_type=jnp.float32,
            )
            picked[rows_at(n, size), :] = product.astype(picked.dtype)
        return carry

    lax.fori_loop(0, (length + UNROLL - 1) // UNROLL, pick, 0)

    def spread(relation, carry):
        start = starts_ref[group * relations + relation]
        end = starts_ref[group * relations + relation + 1]

        def quad(step, carry):
            begin = start + step * QUAD
            for count in range(1, QUAD + 1):
                enough = (end - begin >= count) if count == QUAD else (end - begin == count)

                @pl.when(enough)
                def _():
                    moved = jnp.dot(
                        picked[pl.ds(pl.multiple_of((begin - base) * size, size), count * size), :],
                        weight_ref[relation],
                        preferred_element_type=jnp.float32,
                    )
                    for part in range(count):
                        target = rows_at(codes_ref[begin + part] % 16, size)
                        total[target, :] += moved[part * size : (part + 1) * size]

            return carry

        return lax.fori_loop(0, (end - start + QUAD - 1) // QUAD, quad, carry)

    lax.fori_loop(0, relations, spread, 0)
    if last:
        for d in range(Y):
            for e in range(Z):
                rows = pl.ds((d * Z + e) * size, size)
                y_refs[d][e] = total[rows, :SPLIT].astype(jnp.bfloat16)
                z_refs[e % 2][e // 2, d] = total[rows, SPLIT:].astype(jnp.bfloat16)


def plan_kernel(table_ref, codes_ref, starts_ref):
    relations, slots = table_ref.shape
    row_me, col_me = lax.axis_index("row"), lax.axis_index("col")
    for index in range(4 * relations + 1):
        starts_ref[index] = 0

    def parts(relation, slot):
        packed = table_ref[relation, slot]
        source = (packed >> 4 & 15) ^ row_me
        target = (packed & 15) ^ col_me
        return packed >> 8, (source >> 3) * 2 + (source & 1), source >> 1 & 3, (target & 3) * 4 + (target >> 2)

    def per_slot(act):
        for relation in range(relations):
            live = table_ref[relation, 0] >> 8

            def body(slot, carry):
                at = relation * slots + slot
                _, group, place, target = parts(relation, slot)
                act(group * relations + relation, at, place, target)
                return carry

            lax.fori_loop(0, live, body, 0)

    def count(index, at, place, target):
        starts_ref[index + 1] = starts_ref[index + 1] + 1

    def put(index, at, place, target):
        spot = starts_ref[index]
        codes_ref[spot] = at * 64 + place * 16 + target
        starts_ref[index] = spot + 1

    per_slot(count)
    for index in range(1, 4 * relations + 1):
        starts_ref[index] = starts_ref[index] + starts_ref[index - 1]
    per_slot(put)
    for index in range(4 * relations - 1, 0, -1):
        starts_ref[index] = starts_ref[index - 1]
    starts_ref[0] = 0


def plan(block_rows, block_cols, block_counts):
    relations, slots = block_rows.shape[2:]
    smem = pl.BlockSpec(memory_space=pltpu.SMEM)
    many = relations * slots
    table = (block_rows + block_cols * 16 + block_counts[..., None] * 256)[0, 0]
    return pl.pallas_call(
        plan_kernel,
        out_shape=[
            jax.ShapeDtypeStruct((many,), jnp.int32),
            jax.ShapeDtypeStruct((4 * relations + 1,), jnp.int32),
        ],
        in_specs=[smem],
        out_specs=[smem] * 2,
        compiler_params=pltpu.CompilerParams(vmem_limit_bytes=1 << 20),
        name="plan",
    )(table)


def tile_stage(group, tables, blocks, weights, value, total):
    many, size, _ = blocks.shape
    width = weights.shape[-1]
    first, last = group == 0, group == 3
    vmem = pl.BlockSpec(memory_space=pltpu.VMEM)
    smem = pl.BlockSpec(memory_space=pltpu.SMEM)
    out_shape = [jax.ShapeDtypeStruct((Y * Z * size, width), jnp.float32)]
    if last:
        out_shape += [jax.ShapeDtypeStruct((Z, size, SPLIT), jnp.bfloat16)] * Y
        out_shape += [jax.ShapeDtypeStruct((Z // 2, Y, size, width - SPLIT), jnp.bfloat16)] * 2
    args = [*tables, blocks, weights, value]
    if not first:
        args.append(total)
    return pl.pallas_call(
        functools.partial(stage_kernel, group, first, last),
        out_shape=out_shape,
        in_specs=[smem] * 2 + [vmem] * (len(args) - 2),
        out_specs=[vmem] * len(out_shape),
        scratch_shapes=[pltpu.VMEM((many * size, width), jnp.bfloat16)],
        input_output_aliases={} if first else {len(args) - 1: 0},
        compiler_params=pltpu.CompilerParams(vmem_limit_bytes=14 << 20),
        cost_estimate=pl.CostEstimate(flops=1 << 30, bytes_accessed=4 << 20, transcendentals=0),
        name="tile",
    )(*args)


def small(function, out_shape, *args):
    def kernel(*refs):
        function(refs[: len(args)], refs[len(args) :])

    vmem = pl.BlockSpec(memory_space=pltpu.VMEM)
    return pl.pallas_call(
        kernel,
        out_shape=out_shape,
        in_specs=[vmem] * len(args),
        out_specs=[vmem] * len(out_shape),
        compiler_params=pltpu.CompilerParams(vmem_limit_bytes=4 << 20),
        name="merge",
    )(*args)


def merge_y(ins, outs):
    for e in range(Z):
        summed = sum(ref[e].astype(jnp.float32) for ref in ins)
        outs[e][...] = summed.astype(outs[e].dtype)


def merge_z_near(ins, outs):
    own, got = ins
    outs[0][...] = own[0].astype(jnp.float32) + got[0].astype(jnp.float32)
    outs[1][...] = (own[1].astype(jnp.float32) + got[1].astype(jnp.float32)).astype(jnp.bfloat16)


def merge_z_far(ins, outs):
    kept, got = ins
    for d in range(Y):
        summed = kept[d] + got[d].astype(jnp.float32)
        if d == 0 or d == 3:
            outs[d // 3][...] = summed
        else:
            outs[2][d - 1] = summed.astype(jnp.bfloat16)


def merge_z_last(ins, outs):
    here, across, got = ins
    outs[0][...] = here[...] + got[0].astype(jnp.float32)
    outs[1][...] = (across[...] + got[1].astype(jnp.float32)).astype(jnp.bfloat16)


def load_kernel(blocks_ref, weights_ref, blocks_out, weights_out):
    blocks_out[...] = blocks_ref[...]
    weights_out[...] = weights_ref[...]


def load(blocks, weights):
    vmem = pl.BlockSpec(memory_space=pltpu.VMEM)
    return pl.pallas_call(
        load_kernel,
        out_shape=[jax.ShapeDtypeStruct(a.shape, a.dtype) for a in (blocks, weights)],
        in_specs=[vmem] * 2,
        out_specs=[vmem] * 2,
        compiler_params=pltpu.CompilerParams(vmem_limit_bytes=2 << 20),
        name="load",
    )(blocks, weights)


def gather_groups(features, to_plan, blocks, weights):
    far = row_swap(features, 1, 0, 0)
    near_parts = [features] + [row_swap(features, 0, d, 0) for d in (1, 2, 3)]
    blocks, weights = load(blocks, weights)
    far, blocks, weights, to_plan = lax.optimization_barrier((far, blocks, weights, to_plan))
    tables = plan(*to_plan)
    stage = lambda index, value, total: tile_stage(index, tables, blocks, weights, value, total)
    far_parts = [far] + [row_swap(far, 0, d, 0) for d in (1, 2, 3)]
    near = jnp.concatenate(near_parts, axis=0)
    near_other = row_swap(near, 0, 0, 1)
    (total,) = stage(0, near, None)
    (total,) = stage(1, near_other, total)
    far_parts[-1], total = lax.optimization_barrier((far_parts[-1], total))
    rest = jnp.concatenate(far_parts, axis=0)
    rest_other = row_swap(rest, 0, 0, 1)
    (total,) = stage(2, rest, total)
    return stage(3, rest_other, total)[1:]


def scatter_sum(parts, features, self_weight):
    y_parts, (z_here, z_there) = parts[:Y], parts[Y:]
    f32, bf16 = jnp.float32, jnp.bfloat16
    many, size, columns = z_here.shape[1:]
    piece = (size, columns)
    z_near = col_swap(z_there, 1, 0)
    y_in = [col_swap(y_parts[d], 0, d) for d in (2, 1, 3)]
    shapes = [jax.ShapeDtypeStruct((many, *piece), f32), jax.ShapeDtypeStruct((many, *piece), bf16)]
    z_kept, z_send = small(merge_z_near, shapes, z_here, z_near)
    z_far = col_swap(z_send, 2, 0)
    features, z_kept = lax.optimization_barrier((features, z_kept))
    self_term = jnp.dot(features, self_weight, preferred_element_type=jnp.float32)
    self_term, z_far = lax.optimization_barrier((self_term, z_far))
    shapes = [jax.ShapeDtypeStruct(piece, f32)] * 2 + [jax.ShapeDtypeStruct((2, *piece), bf16)]
    z_own, z_across, z_send = small(merge_z_far, shapes, z_kept, z_far)
    z_got = col_swap(z_send, 0, 1)
    y_in, z_across = lax.optimization_barrier((y_in, z_across))
    piece_y = y_parts[0].shape[1:]
    shapes = [jax.ShapeDtypeStruct(piece_y, f32)] + [jax.ShapeDtypeStruct(piece_y, bf16)] * 3
    y_own, *y_send = small(merge_y, shapes, y_parts[0], *y_in)
    y_last = [col_swap(y_send[e - 1], e, 0) for e in (2, 3, 1)]
    shapes = [jax.ShapeDtypeStruct(piece, f32), jax.ShapeDtypeStruct(piece, bf16)]
    z_got, y_own = lax.optimization_barrier((z_got, y_own))
    z_own, z_send = small(merge_z_last, shapes, z_own, z_across, z_got)
    z_own += col_swap(z_send, 0, 3).astype(f32)
    y_last, z_own = lax.optimization_barrier((y_last, z_own))
    y_own += sum(part.astype(f32) for part in y_last)
    return y_own, z_own, self_term


def per_device(
    features, self_weight, rel_weight, bias, blocks, block_rows, block_cols, block_counts
):
    relations, slots, size, _ = blocks.shape[2:]
    weights = jnp.transpose(rel_weight, (1, 0, 2))
    blocks = blocks.reshape(relations * slots, size, size)
    to_plan = (block_rows, block_cols, block_counts)
    parts = gather_groups(features, to_plan, blocks, weights)
    y_own, z_own, self_term = scatter_sum(parts, features, self_weight)
    owned = jnp.concatenate([y_own, z_own], axis=1)
    return jnp.maximum(self_term + owned + bias, 0.0).astype(jnp.bfloat16)


def solution(mesh):
    return jax.shard_map(
        per_device,
        mesh=mesh,
        in_specs=(
            P(("row", "col"), None),
            P(),
            P(),
            P(),
            P("row", "col", None, None, None, None),
            P("row", "col", None, None),
            P("row", "col", None, None),
            P("row", "col", None),
        ),
        out_specs=P(("row", "col"), None),
        check_vma=False,
    )
```

```python
import functools

import jax
import jax.numpy as jnp
from jax import lax
from jax.experimental import pallas as pl
from jax.experimental.pallas import tpu as pltpu
from jax.sharding import PartitionSpec as P

Z, Y = 4, 4
SPLIT = 512
UNROLL, QUAD = 4, 4


def row_swap(value, dz, dx, dc):
    return lax.ppermute(value, "row", [(at, at ^ (dz * 8 + dx * 2 + dc)) for at in range(16)])


def col_swap(value, dz, dy):
    return lax.ppermute(value, "col", [(at, at ^ (dz * Y + dy)) for at in range(16)])


def rows_at(index, size):
    return pl.ds(pl.multiple_of(index * size, size), size)


def stage_kernel(group, first, last, codes_ref, starts_ref, blocks_ref, weight_ref, group_ref, *refs):
    if not first:
        refs = refs[1:]
    total, refs = refs[0], refs[1:]
    if last:
        y_refs, z_refs, refs = refs[:Y], refs[Y : Y + 2], refs[Y + 2 :]
    (picked,) = refs
    relations = weight_ref.shape[0]
    size = blocks_ref.shape[-1]
    if first:
        total[...] = jnp.zeros_like(total)
    base = starts_ref[group * relations]
    length = starts_ref[(group + 1) * relations] - base

    def pick(step, carry):
        for u in range(UNROLL):
            n = jnp.minimum(step * UNROLL + u, length - 1)
            code = codes_ref[base + n]
            product = jnp.dot(
                blocks_ref[code // 64],
                group_ref[rows_at(code // 16 % 4, size), :],
                preferred_element_type=jnp.float32,
            )
            picked[rows_at(n, size), :] = product.astype(picked.dtype)
        return carry

    lax.fori_loop(0, (length + UNROLL - 1) // UNROLL, pick, 0)

    def spread(relation, carry):
        start = starts_ref[group * relations + relation]
        end = starts_ref[group * relations + relation + 1]

        def quad(step, carry):
            begin = start + step * QUAD
            for count in range(1, QUAD + 1):
                enough = (end - begin >= count) if count == QUAD else (end - begin == count)

                @pl.when(enough)
                def _():
                    moved = jnp.dot(
                        picked[pl.ds(pl.multiple_of((begin - base) * size, size), count * size), :],
                        weight_ref[relation],
                        preferred_element_type=jnp.float32,
                    )
                    for part in range(count):
                        target = rows_at(codes_ref[begin + part] % 16, size)
                        total[target, :] += moved[part * size : (part + 1) * size]

            return carry

        return lax.fori_loop(0, (end - start + QUAD - 1) // QUAD, quad, carry)

    lax.fori_loop(0, relations, spread, 0)
    if last:
        for d in range(Y):
            for e in range(Z):
                rows = pl.ds((d * Z + e) * size, size)
                y_refs[d][e] = total[rows, :SPLIT].astype(jnp.bfloat16)
                z_refs[e % 2][e // 2, d] = total[rows, SPLIT:].astype(jnp.bfloat16)


def plan_kernel(table_ref, codes_ref, starts_ref):
    relations, slots = table_ref.shape
    row_me, col_me = lax.axis_index("row"), lax.axis_index("col")
    for index in range(4 * relations + 1):
        starts_ref[index] = 0

    def parts(relation, slot):
        packed = table_ref[relation, slot]
        source = (packed >> 4 & 15) ^ row_me
        target = (packed & 15) ^ col_me
        return packed >> 8, (source >> 3) * 2 + (source & 1), source >> 1 & 3, (target & 3) * 4 + (target >> 2)

    def per_slot(act):
        for relation in range(relations):
            live = table_ref[relation, 0] >> 8

            def body(slot, carry):
                at = relation * slots + slot
                _, group, place, target = parts(relation, slot)
                act(group * relations + relation, at, place, target)
                return carry

            lax.fori_loop(0, live, body, 0)

    def count(index, at, place, target):
        starts_ref[index + 1] = starts_ref[index + 1] + 1

    def put(index, at, place, target):
        spot = starts_ref[index]
        codes_ref[spot] = at * 64 + place * 16 + target
        starts_ref[index] = spot + 1

    per_slot(count)
    for index in range(1, 4 * relations + 1):
        starts_ref[index] = starts_ref[index] + starts_ref[index - 1]
    per_slot(put)
    for index in range(4 * relations - 1, 0, -1):
        starts_ref[index] = starts_ref[index - 1]
    starts_ref[0] = 0


def plan(block_rows, block_cols, block_counts):
    relations, slots = block_rows.shape[2:]
    smem = pl.BlockSpec(memory_space=pltpu.SMEM)
    many = relations * slots
    table = (block_rows + block_cols * 16 + block_counts[..., None] * 256)[0, 0]
    return pl.pallas_call(
        plan_kernel,
        out_shape=[
            jax.ShapeDtypeStruct((many,), jnp.int32),
            jax.ShapeDtypeStruct((4 * relations + 1,), jnp.int32),
        ],
        in_specs=[smem],
        out_specs=[smem] * 2,
        compiler_params=pltpu.CompilerParams(vmem_limit_bytes=1 << 20),
        name="plan",
    )(table)


def tile_stage(group, tables, blocks, weights, value, total):
    many, size, _ = blocks.shape
    width = weights.shape[-1]
    first, last = group == 0, group == 3
    vmem = pl.BlockSpec(memory_space=pltpu.VMEM)
    smem = pl.BlockSpec(memory_space=pltpu.SMEM)
    out_shape = [jax.ShapeDtypeStruct((Y * Z * size, width), jnp.float32)]
    if last:
        out_shape += [jax.ShapeDtypeStruct((Z, size, SPLIT), jnp.bfloat16)] * Y
        out_shape += [jax.ShapeDtypeStruct((Z // 2, Y, size, width - SPLIT), jnp.bfloat16)] * 2
    args = [*tables, blocks, weights, value]
    if not first:
        args.append(total)
    return pl.pallas_call(
        functools.partial(stage_kernel, group, first, last),
        out_shape=out_shape,
        in_specs=[smem] * 2 + [vmem] * (len(args) - 2),
        out_specs=[vmem] * len(out_shape),
        scratch_shapes=[pltpu.VMEM((many * size, width), jnp.bfloat16)],
        input_output_aliases={} if first else {len(args) - 1: 0},
        compiler_params=pltpu.CompilerParams(vmem_limit_bytes=14 << 20),
        cost_estimate=pl.CostEstimate(flops=1 << 30, bytes_accessed=4 << 20, transcendentals=0),
        name="tile",
    )(*args)


def small(function, out_shape, *args):
    def kernel(*refs):
        function(refs[: len(args)], refs[len(args) :])

    vmem = pl.BlockSpec(memory_space=pltpu.VMEM)
    return pl.pallas_call(
        kernel,
        out_shape=out_shape,
        in_specs=[vmem] * len(args),
        out_specs=[vmem] * len(out_shape),
        compiler_params=pltpu.CompilerParams(vmem_limit_bytes=4 << 20),
        name="merge",
    )(*args)


def merge_y(ins, outs):
    for e in range(Z):
        summed = sum(ref[e].astype(jnp.float32) for ref in ins)
        outs[e][...] = summed.astype(outs[e].dtype)


def merge_z_near(ins, outs):
    own, got = ins
    outs[0][...] = own[0].astype(jnp.float32) + got[0].astype(jnp.float32)
    outs[1][...] = (own[1].astype(jnp.float32) + got[1].astype(jnp.float32)).astype(jnp.bfloat16)


def merge_z_far(ins, outs):
    kept, got = ins
    for d in range(Y):
        summed = kept[d] + got[d].astype(jnp.float32)
        if d == 0 or d == 3:
            outs[d // 3][...] = summed
        else:
            outs[2][d - 1] = summed.astype(jnp.bfloat16)


def merge_z_last(ins, outs):
    here, across, got = ins
    outs[0][...] = here[...] + got[0].astype(jnp.float32)
    outs[1][...] = (across[...] + got[1].astype(jnp.float32)).astype(jnp.bfloat16)


def load_kernel(blocks_ref, weights_ref, blocks_out, weights_out):
    blocks_out[...] = blocks_ref[...]
    weights_out[...] = weights_ref[...]


def load(blocks, weights):
    vmem = pl.BlockSpec(memory_space=pltpu.VMEM)
    return pl.pallas_call(
        load_kernel,
        out_shape=[jax.ShapeDtypeStruct(a.shape, a.dtype) for a in (blocks, weights)],
        in_specs=[vmem] * 2,
        out_specs=[vmem] * 2,
        compiler_params=pltpu.CompilerParams(vmem_limit_bytes=2 << 20),
        name="load",
    )(blocks, weights)


def gather_groups(features, to_plan, blocks, weights):
    far = row_swap(features, 1, 0, 0)
    near_parts = [features] + [row_swap(features, 0, d, 0) for d in (1, 2, 3)]
    blocks, weights = load(blocks, weights)
    far, blocks, weights, to_plan = lax.optimization_barrier((far, blocks, weights, to_plan))
    tables = plan(*to_plan)
    stage = lambda index, value, total: tile_stage(index, tables, blocks, weights, value, total)
    far_parts = [far] + [row_swap(far, 0, d, 0) for d in (1, 2, 3)]
    near = jnp.concatenate(near_parts, axis=0)
    near_other = row_swap(near, 0, 0, 1)
    (total,) = stage(0, near, None)
    (total,) = stage(1, near_other, total)
    far_parts[-1], total = lax.optimization_barrier((far_parts[-1], total))
    rest = jnp.concatenate(far_parts, axis=0)
    rest_other = row_swap(rest, 0, 0, 1)
    (total,) = stage(2, rest, total)
    return stage(3, rest_other, total)[1:]


def scatter_sum(parts, features, self_weight):
    y_parts, (z_here, z_there) = parts[:Y], parts[Y:]
    f32, bf16 = jnp.float32, jnp.bfloat16
    many, size, columns = z_here.shape[1:]
    piece = (size, columns)
    z_near = col_swap(z_there, 1, 0)
    y_in = [col_swap(y_parts[d], 0, d) for d in (2, 1, 3)]
    shapes = [jax.ShapeDtypeStruct((many, *piece), f32), jax.ShapeDtypeStruct((many, *piece), bf16)]
    z_kept, z_send = small(merge_z_near, shapes, z_here, z_near)
    z_far = col_swap(z_send, 2, 0)
    features, z_kept = lax.optimization_barrier((features, z_kept))
    self_term = jnp.dot(features, self_weight, preferred_element_type=jnp.float32)
    self_term, z_far = lax.optimization_barrier((self_term, z_far))
    shapes = [jax.ShapeDtypeStruct(piece, f32)] * 2 + [jax.ShapeDtypeStruct((2, *piece), bf16)]
    z_own, z_across, z_send = small(merge_z_far, shapes, z_kept, z_far)
    z_got = col_swap(z_send, 0, 1)
    y_in, z_across = lax.optimization_barrier((y_in, z_across))
    piece_y = y_parts[0].shape[1:]
    shapes = [jax.ShapeDtypeStruct(piece_y, f32)] + [jax.ShapeDtypeStruct(piece_y, bf16)] * 3
    y_own, *y_send = small(merge_y, shapes, y_parts[0], *y_in)
    y_last = [col_swap(y_send[e - 1], e, 0) for e in (2, 3, 1)]
    shapes = [jax.ShapeDtypeStruct(piece, f32), jax.ShapeDtypeStruct(piece, bf16)]
    z_got, y_own = lax.optimization_barrier((z_got, y_own))
    z_own, z_send = small(merge_z_last, shapes, z_own, z_across, z_got)
    z_last = col_swap(z_send, 0, 3)
    y_own += sum(part.astype(f32) for part in y_last)
    z_last, y_own = lax.optimization_barrier((z_last, y_own))
    z_own += z_last.astype(f32)
    return y_own, z_own, self_term


def per_device(
    features, self_weight, rel_weight, bias, blocks, block_rows, block_cols, block_counts
):
    relations, slots, size, _ = blocks.shape[2:]
    weights = jnp.transpose(rel_weight, (1, 0, 2))
    blocks = blocks.reshape(relations * slots, size, size)
    to_plan = (block_rows, block_cols, block_counts)
    parts = gather_groups(features, to_plan, blocks, weights)
    y_own, z_own, self_term = scatter_sum(parts, features, self_weight)
    owned = jnp.concatenate([y_own, z_own], axis=1)
    return jnp.maximum(self_term + owned + bias, 0.0).astype(jnp.bfloat16)


def solution(mesh):
    return jax.shard_map(
        per_device,
        mesh=mesh,
        in_specs=(
            P(("row", "col"), None),
            P(),
            P(),
            P(),
            P("row", "col", None, None, None, None),
            P("row", "col", None, None),
            P("row", "col", None, None),
            P("row", "col", None),
        ),
        out_specs=P(("row", "col"), None),
        check_vma=False,
    )
```

```python
import functools

import jax
import jax.numpy as jnp
from jax import lax
from jax.experimental import pallas as pl
from jax.experimental.pallas import tpu as pltpu
from jax.sharding import PartitionSpec as P

Z, Y = 4, 4
FIRST = 32
UNROLL, QUAD = 4, 4


def row_swap(value, dz, dx, dc):
    return lax.ppermute(value, "row", [(at, at ^ (dz * 8 + dx * 2 + dc)) for at in range(16)])


def col_swap(value, dz, dy):
    return lax.ppermute(value, "col", [(at, at ^ (dz * Y + dy)) for at in range(16)])


def rows_at(index, size):
    return pl.ds(pl.multiple_of(index * size, size), size)


def stage_kernel(group, first, last, codes_ref, starts_ref, blocks_ref, weight_ref, group_ref, *refs):
    if not first:
        refs = refs[1:]
    total, refs = refs[0], refs[1:]
    if last:
        y_refs, z_refs, own_ref, refs = refs[:Y], refs[Y : Y + 2], refs[Y + 2], refs[Y + 3 :]
    (picked,) = refs
    relations = weight_ref.shape[0]
    size = blocks_ref.shape[-1]
    if first:
        total[...] = jnp.zeros_like(total)
    base = starts_ref[group * relations]
    length = starts_ref[(group + 1) * relations] - base

    def pick(step, carry):
        for u in range(UNROLL):
            n = jnp.minimum(step * UNROLL + u, length - 1)
            code = codes_ref[base + n]
            product = jnp.dot(
                blocks_ref[code // 64],
                group_ref[rows_at(code // 16 % 4, size), :],
                preferred_element_type=jnp.float32,
            )
            picked[rows_at(n, size), :] = product.astype(picked.dtype)
        return carry

    lax.fori_loop(0, (length + UNROLL - 1) // UNROLL, pick, 0)

    def spread(relation, carry):
        start = starts_ref[group * relations + relation]
        end = starts_ref[group * relations + relation + 1]

        def quad(step, carry):
            begin = start + step * QUAD
            for count in range(1, QUAD + 1):
                enough = (end - begin >= count) if count == QUAD else (end - begin == count)

                @pl.when(enough)
                def _():
                    moved = jnp.dot(
                        picked[pl.ds(pl.multiple_of((begin - base) * size, size), count * size), :],
                        weight_ref[relation],
                        preferred_element_type=jnp.float32,
                    )
                    for part in range(count):
                        target = rows_at(codes_ref[begin + part] % 16, size)
                        total[target, :] += moved[part * size : (part + 1) * size]

            return carry

        return lax.fori_loop(0, (end - start + QUAD - 1) // QUAD, quad, carry)

    lax.fori_loop(0, relations, spread, 0)
    if last:
        for d in range(Y):
            for e in range(Z):
                rows = total[(d * Z + e) * size : (d * Z + e + 1) * size, :].astype(jnp.bfloat16)
                z_refs[e % 2][e // 2, d] = rows[:FIRST]
                if e == 0:
                    own_ref[d] = rows[FIRST:]
                else:
                    y_refs[d][e - 1] = rows[FIRST:]


def plan_kernel(table_ref, codes_ref, starts_ref):
    relations, slots = table_ref.shape
    row_me, col_me = lax.axis_index("row"), lax.axis_index("col")
    for index in range(4 * relations + 1):
        starts_ref[index] = 0

    def parts(relation, slot):
        packed = table_ref[relation, slot]
        source = (packed >> 4 & 15) ^ row_me
        target = (packed & 15) ^ col_me
        return packed >> 8, (source >> 3) * 2 + (source & 1), source >> 1 & 3, (target & 3) * 4 + (target >> 2)

    def per_slot(act):
        for relation in range(relations):
            live = table_ref[relation, 0] >> 8

            def body(slot, carry):
                at = relation * slots + slot
                _, group, place, target = parts(relation, slot)
                act(group * relations + relation, at, place, target)
                return carry

            lax.fori_loop(0, live, body, 0)

    def count(index, at, place, target):
        starts_ref[index + 1] = starts_ref[index + 1] + 1

    def put(index, at, place, target):
        spot = starts_ref[index]
        codes_ref[spot] = at * 64 + place * 16 + target
        starts_ref[index] = spot + 1

    per_slot(count)
    for index in range(1, 4 * relations + 1):
        starts_ref[index] = starts_ref[index] + starts_ref[index - 1]
    per_slot(put)
    for index in range(4 * relations - 1, 0, -1):
        starts_ref[index] = starts_ref[index - 1]
    starts_ref[0] = 0


def plan(block_rows, block_cols, block_counts):
    relations, slots = block_rows.shape[2:]
    smem = pl.BlockSpec(memory_space=pltpu.SMEM)
    many = relations * slots
    table = (block_rows + block_cols * 16 + block_counts[..., None] * 256)[0, 0]
    return pl.pallas_call(
        plan_kernel,
        out_shape=[
            jax.ShapeDtypeStruct((many,), jnp.int32),
            jax.ShapeDtypeStruct((4 * relations + 1,), jnp.int32),
        ],
        in_specs=[smem],
        out_specs=[smem] * 2,
        compiler_params=pltpu.CompilerParams(vmem_limit_bytes=1 << 20),
        name="plan",
    )(table)


def tile_stage(group, tables, blocks, weights, value, total):
    many, size, _ = blocks.shape
    width = weights.shape[-1]
    first, last = group == 0, group == 3
    vmem = pl.BlockSpec(memory_space=pltpu.VMEM)
    smem = pl.BlockSpec(memory_space=pltpu.SMEM)
    out_shape = [jax.ShapeDtypeStruct((Y * Z * size, width), jnp.float32)]
    if last:
        out_shape += [jax.ShapeDtypeStruct((Z - 1, size - FIRST, width), jnp.bfloat16)] * Y
        out_shape += [jax.ShapeDtypeStruct((Z // 2, Y, FIRST, width), jnp.bfloat16)] * 2
        out_shape += [jax.ShapeDtypeStruct((Y, size - FIRST, width), jnp.bfloat16)]
    args = [*tables, blocks, weights, value]
    if not first:
        args.append(total)
    return pl.pallas_call(
        functools.partial(stage_kernel, group, first, last),
        out_shape=out_shape,
        in_specs=[smem] * 2 + [vmem] * (len(args) - 2),
        out_specs=[vmem] * len(out_shape),
        scratch_shapes=[pltpu.VMEM((many * size, width), jnp.bfloat16)],
        input_output_aliases={} if first else {len(args) - 1: 0},
        compiler_params=pltpu.CompilerParams(vmem_limit_bytes=14 << 20),
        cost_estimate=pl.CostEstimate(flops=1 << 30, bytes_accessed=4 << 20, transcendentals=0),
        name="tile",
    )(*args)


def small(function, out_shape, *args):
    def kernel(*refs):
        function(refs[: len(args)], refs[len(args) :])

    vmem = pl.BlockSpec(memory_space=pltpu.VMEM)
    return pl.pallas_call(
        kernel,
        out_shape=out_shape,
        in_specs=[vmem] * len(args),
        out_specs=[vmem] * len(out_shape),
        compiler_params=pltpu.CompilerParams(vmem_limit_bytes=4 << 20),
        name="merge",
    )(*args)


def merge_y(ins, outs):
    for e in range(Z - 1):
        outs[e][...] = sum(ref[e].astype(jnp.float32) for ref in ins).astype(jnp.bfloat16)


def merge_z_near(ins, outs):
    own, got = ins
    outs[0][...] = own[0].astype(jnp.float32) + got[0].astype(jnp.float32)
    outs[1][...] = (own[1].astype(jnp.float32) + got[1].astype(jnp.float32)).astype(jnp.bfloat16)


def merge_z_far(ins, outs):
    kept, got, own = ins
    for d in range(Y):
        top = kept[d] + got[d].astype(jnp.float32)
        if d == 0 or d == 3:
            outs[d // 3][:FIRST, :] = top
            outs[d // 3][FIRST:, :] = own[d].astype(jnp.float32)
        else:
            outs[2][d - 1, :FIRST, :] = top.astype(jnp.bfloat16)
            outs[2][d - 1, FIRST:, :] = own[d]


def merge_z_last(ins, outs):
    here, across, got = ins
    outs[0][...] = here[...] + got[0].astype(jnp.float32)
    outs[1][...] = (across[...] + got[1].astype(jnp.float32)).astype(jnp.bfloat16)


def load_kernel(blocks_ref, weights_ref, blocks_out, weights_out):
    blocks_out[...] = blocks_ref[...]
    weights_out[...] = weights_ref[...]


def load(blocks, weights):
    vmem = pl.BlockSpec(memory_space=pltpu.VMEM)
    return pl.pallas_call(
        load_kernel,
        out_shape=[jax.ShapeDtypeStruct(a.shape, a.dtype) for a in (blocks, weights)],
        in_specs=[vmem] * 2,
        out_specs=[vmem] * 2,
        compiler_params=pltpu.CompilerParams(vmem_limit_bytes=2 << 20),
        name="load",
    )(blocks, weights)


def gather_groups(features, to_plan, blocks, weights):
    far = row_swap(features, 1, 0, 0)
    near_parts = [features] + [row_swap(features, 0, d, 0) for d in (1, 2, 3)]
    blocks, weights = load(blocks, weights)
    far, blocks, weights, to_plan = lax.optimization_barrier((far, blocks, weights, to_plan))
    tables = plan(*to_plan)
    stage = lambda index, value, total: tile_stage(index, tables, blocks, weights, value, total)
    far_parts = [far] + [row_swap(far, 0, d, 0) for d in (1, 2, 3)]
    near = jnp.concatenate(near_parts, axis=0)
    near_other = row_swap(near, 0, 0, 1)
    (total,) = stage(0, near, None)
    (total,) = stage(1, near_other, total)
    far_parts[-1], total = lax.optimization_barrier((far_parts[-1], total))
    rest = jnp.concatenate(far_parts, axis=0)
    rest_other = row_swap(rest, 0, 0, 1)
    (total,) = stage(2, rest, total)
    return stage(3, rest_other, total)[1:]


def scatter_sum(parts, features, self_weight):
    y_parts, (z_here, z_there, own) = parts[:Y], parts[Y:]
    f32, bf16 = jnp.float32, jnp.bfloat16
    width = own.shape[-1]
    z_near = col_swap(z_there, 1, 0)
    y_in = [col_swap(y_parts[d], 0, d) for d in (2, 1, 3)]
    piece = z_here.shape[1:]
    shapes = [jax.ShapeDtypeStruct(piece, f32), jax.ShapeDtypeStruct(piece, bf16)]
    z_kept, z_send = small(merge_z_near, shapes, z_here, z_near)
    z_far = col_swap(z_send, 2, 0)
    features, z_kept = lax.optimization_barrier((features, z_kept))
    self_term = jnp.dot(features, self_weight, preferred_element_type=f32)
    self_term, z_far = lax.optimization_barrier((self_term, z_far))
    block = (FIRST + own.shape[1], width)
    shapes = [jax.ShapeDtypeStruct(block, f32)] * 2 + [jax.ShapeDtypeStruct((2, *block), bf16)]
    here, across, send = small(merge_z_far, shapes, z_kept, z_far, own)
    got = col_swap(send, 0, 1)
    y_in, across = lax.optimization_barrier((y_in, across))
    shapes = [jax.ShapeDtypeStruct(own.shape[1:], bf16)] * (Z - 1)
    y_send = list(small(merge_y, shapes, y_parts[0], *y_in))
    y_last = [col_swap(y_send[e - 1], e, 0) for e in (2, 3, 1)]
    y_send[0], got = lax.optimization_barrier((y_send[0], got))
    shapes = [jax.ShapeDtypeStruct(block, f32), jax.ShapeDtypeStruct(block, bf16)]
    here, send = small(merge_z_last, shapes, here, across, got)
    last = col_swap(send, 0, 3)
    y_sum = sum(part.astype(f32) for part in y_last)
    last, y_sum = lax.optimization_barrier((last, y_sum))
    here += last.astype(f32)
    return jnp.concatenate([here[:FIRST], here[FIRST:] + y_sum], axis=0), self_term


def per_device(
    features, self_weight, rel_weight, bias, blocks, block_rows, block_cols, block_counts
):
    relations, slots, size, _ = blocks.shape[2:]
    weights = jnp.transpose(rel_weight, (1, 0, 2))
    blocks = blocks.reshape(relations * slots, size, size)
    to_plan = (block_rows, block_cols, block_counts)
    parts = gather_groups(features, to_plan, blocks, weights)
    owned, self_term = scatter_sum(parts, features, self_weight)
    return jnp.maximum(self_term + owned + bias, 0.0).astype(jnp.bfloat16)


def solution(mesh):
    return jax.shard_map(
        per_device,
        mesh=mesh,
        in_specs=(
            P(("row", "col"), None),
            P(),
            P(),
            P(),
            P("row", "col", None, None, None, None),
            P("row", "col", None, None),
            P("row", "col", None, None),
            P("row", "col", None),
        ),
        out_specs=P(("row", "col"), None),
        check_vma=False,
    )
```

```python
import functools

import jax
import jax.numpy as jnp
from jax import lax
from jax.experimental import pallas as pl
from jax.experimental.pallas import tpu as pltpu
from jax.sharding import PartitionSpec as P

Z, Y = 4, 4
FIRST = 32
UNROLL, QUAD = 4, 4


def row_swap(value, dz, dx, dc):
    return lax.ppermute(value, "row", [(at, at ^ (dz * 8 + dx * 2 + dc)) for at in range(16)])


def col_swap(value, dz, dy):
    return lax.ppermute(value, "col", [(at, at ^ (dz * Y + dy)) for at in range(16)])


def rows_at(index, size):
    return pl.ds(pl.multiple_of(index * size, size), size)


def stage_kernel(group, first, last, codes_ref, starts_ref, blocks_ref, weight_ref, group_ref, *refs):
    if not first:
        refs = refs[1:]
    total, refs = refs[0], refs[1:]
    if last:
        y_refs, z_refs, own_ref, refs = refs[:Y], refs[Y : Y + 2], refs[Y + 2], refs[Y + 3 :]
    (picked,) = refs
    relations = weight_ref.shape[0]
    size = blocks_ref.shape[-1]
    if first:
        total[...] = jnp.zeros_like(total)
    base = starts_ref[group * relations]
    length = starts_ref[(group + 1) * relations] - base

    def pick(step, carry):
        for u in range(UNROLL):
            n = jnp.minimum(step * UNROLL + u, length - 1)
            code = codes_ref[base + n]
            product = jnp.dot(
                blocks_ref[code // 64],
                group_ref[rows_at(code // 16 % 4, size), :],
                preferred_element_type=jnp.float32,
            )
            picked[rows_at(n, size), :] = product.astype(picked.dtype)
        return carry

    lax.fori_loop(0, (length + UNROLL - 1) // UNROLL, pick, 0)

    def spread(relation, carry):
        start = starts_ref[group * relations + relation]
        end = starts_ref[group * relations + relation + 1]

        def quad(step, carry):
            begin = start + step * QUAD
            for count in range(1, QUAD + 1):
                enough = (end - begin >= count) if count == QUAD else (end - begin == count)

                @pl.when(enough)
                def _():
                    moved = jnp.dot(
                        picked[pl.ds(pl.multiple_of((begin - base) * size, size), count * size), :],
                        weight_ref[relation],
                        preferred_element_type=jnp.float32,
                    )
                    for part in range(count):
                        target = rows_at(codes_ref[begin + part] % 16, size)
                        total[target, :] += moved[part * size : (part + 1) * size]

            return carry

        return lax.fori_loop(0, (end - start + QUAD - 1) // QUAD, quad, carry)

    lax.fori_loop(0, relations, spread, 0)
    if last:
        for d in range(Y):
            for e in range(Z):
                rows = total[(d * Z + e) * size : (d * Z + e + 1) * size, :].astype(jnp.bfloat16)
                z_refs[e % 2][e // 2, d] = rows[:FIRST]
                if e == 0:
                    own_ref[d] = rows[FIRST:]
                else:
                    y_refs[d][e - 1] = rows[FIRST:]


def plan_kernel(table_ref, codes_ref, starts_ref):
    relations, slots = table_ref.shape
    row_me, col_me = lax.axis_index("row"), lax.axis_index("col")
    for index in range(4 * relations + 1):
        starts_ref[index] = 0

    def parts(relation, slot):
        packed = table_ref[relation, slot]
        source = (packed >> 4 & 15) ^ row_me
        target = (packed & 15) ^ col_me
        return packed >> 8, (source >> 3) * 2 + (source & 1), (source >> 1 & 3) ^ (source >> 2 & 1), (target & 3) * 4 + (target >> 2)

    def per_slot(act):
        for relation in range(relations):
            live = table_ref[relation, 0] >> 8

            def body(slot, carry):
                at = relation * slots + slot
                _, group, place, target = parts(relation, slot)
                act(group * relations + relation, at, place, target)
                return carry

            lax.fori_loop(0, live, body, 0)

    def count(index, at, place, target):
        starts_ref[index + 1] = starts_ref[index + 1] + 1

    def put(index, at, place, target):
        spot = starts_ref[index]
        codes_ref[spot] = at * 64 + place * 16 + target
        starts_ref[index] = spot + 1

    per_slot(count)
    for index in range(1, 4 * relations + 1):
        starts_ref[index] = starts_ref[index] + starts_ref[index - 1]
    per_slot(put)
    for index in range(4 * relations - 1, 0, -1):
        starts_ref[index] = starts_ref[index - 1]
    starts_ref[0] = 0


def plan(block_rows, block_cols, block_counts):
    relations, slots = block_rows.shape[2:]
    smem = pl.BlockSpec(memory_space=pltpu.SMEM)
    many = relations * slots
    table = (block_rows + block_cols * 16 + block_counts[..., None] * 256)[0, 0]
    return pl.pallas_call(
        plan_kernel,
        out_shape=[
            jax.ShapeDtypeStruct((many,), jnp.int32),
            jax.ShapeDtypeStruct((4 * relations + 1,), jnp.int32),
        ],
        in_specs=[smem],
        out_specs=[smem] * 2,
        compiler_params=pltpu.CompilerParams(vmem_limit_bytes=1 << 20),
        name="plan",
    )(table)


def tile_stage(group, tables, blocks, weights, value, total):
    many, size, _ = blocks.shape
    width = weights.shape[-1]
    first, last = group == 0, group == 3
    vmem = pl.BlockSpec(memory_space=pltpu.VMEM)
    smem = pl.BlockSpec(memory_space=pltpu.SMEM)
    out_shape = [jax.ShapeDtypeStruct((Y * Z * size, width), jnp.float32)]
    if last:
        out_shape += [jax.ShapeDtypeStruct((Z - 1, size - FIRST, width), jnp.bfloat16)] * Y
        out_shape += [jax.ShapeDtypeStruct((Z // 2, Y, FIRST, width), jnp.bfloat16)] * 2
        out_shape += [jax.ShapeDtypeStruct((Y, size - FIRST, width), jnp.bfloat16)]
    args = [*tables, blocks, weights, value]
    if not first:
        args.append(total)
    return pl.pallas_call(
        functools.partial(stage_kernel, group, first, last),
        out_shape=out_shape,
        in_specs=[smem] * 2 + [vmem] * (len(args) - 2),
        out_specs=[vmem] * len(out_shape),
        scratch_shapes=[pltpu.VMEM((many * size, width), jnp.bfloat16)],
        input_output_aliases={} if first else {len(args) - 1: 0},
        compiler_params=pltpu.CompilerParams(vmem_limit_bytes=14 << 20),
        cost_estimate=pl.CostEstimate(flops=1 << 30, bytes_accessed=4 << 20, transcendentals=0),
        name="tile",
    )(*args)


def small(function, out_shape, *args):
    def kernel(*refs):
        function(refs[: len(args)], refs[len(args) :])

    vmem = pl.BlockSpec(memory_space=pltpu.VMEM)
    return pl.pallas_call(
        kernel,
        out_shape=out_shape,
        in_specs=[vmem] * len(args),
        out_specs=[vmem] * len(out_shape),
        compiler_params=pltpu.CompilerParams(vmem_limit_bytes=4 << 20),
        name="merge",
    )(*args)


def merge_y(ins, outs):
    for e in range(Z - 1):
        outs[e][...] = sum(ref[e].astype(jnp.float32) for ref in ins).astype(jnp.bfloat16)


def merge_z_near(ins, outs):
    own, got = ins
    outs[0][...] = own[0].astype(jnp.float32) + got[0].astype(jnp.float32)
    outs[1][...] = (own[1].astype(jnp.float32) + got[1].astype(jnp.float32)).astype(jnp.bfloat16)


def merge_z_far(ins, outs):
    kept, got, own = ins
    for d in range(Y):
        top = kept[d] + got[d].astype(jnp.float32)
        if d == 0 or d == 3:
            outs[d // 3][:FIRST, :] = top
            outs[d // 3][FIRST:, :] = own[d].astype(jnp.float32)
        else:
            outs[2][d - 1, :FIRST, :] = top.astype(jnp.bfloat16)
            outs[2][d - 1, FIRST:, :] = own[d]


def merge_z_last(ins, outs):
    here, across, got = ins
    outs[0][...] = here[...] + got[0].astype(jnp.float32)
    outs[1][...] = (across[...] + got[1].astype(jnp.float32)).astype(jnp.bfloat16)


def load_kernel(blocks_ref, weights_ref, blocks_out, weights_out):
    blocks_out[...] = blocks_ref[...]
    weights_out[...] = weights_ref[...]


def load(blocks, weights):
    vmem = pl.BlockSpec(memory_space=pltpu.VMEM)
    return pl.pallas_call(
        load_kernel,
        out_shape=[jax.ShapeDtypeStruct(a.shape, a.dtype) for a in (blocks, weights)],
        in_specs=[vmem] * 2,
        out_specs=[vmem] * 2,
        compiler_params=pltpu.CompilerParams(vmem_limit_bytes=2 << 20),
        name="load",
    )(blocks, weights)


def gather_groups(features, to_plan, blocks, weights):
    far = row_swap(features, 1, 0, 0)
    near_parts = [features] + [row_swap(features, 0, d, 0) for d in (1, 3, 2)]
    blocks, weights = load(blocks, weights)
    far, blocks, weights, to_plan = lax.optimization_barrier((far, blocks, weights, to_plan))
    tables = plan(*to_plan)
    stage = lambda index, value, total: tile_stage(index, tables, blocks, weights, value, total)
    far_parts = [far] + [row_swap(far, 0, d, 0) for d in (1, 3, 2)]
    near = jnp.concatenate(near_parts, axis=0)
    near_other = row_swap(near, 0, 0, 1)
    (total,) = stage(0, near, None)
    (total,) = stage(1, near_other, total)
    far_parts[-1], total = lax.optimization_barrier((far_parts[-1], total))
    rest = jnp.concatenate(far_parts, axis=0)
    rest_other = row_swap(rest, 0, 0, 1)
    (total,) = stage(2, rest, total)
    return stage(3, rest_other, total)[1:]


def scatter_sum(parts, features, self_weight):
    y_parts, (z_here, z_there, own) = parts[:Y], parts[Y:]
    f32, bf16 = jnp.float32, jnp.bfloat16
    width = own.shape[-1]
    z_near = col_swap(z_there, 1, 0)
    y_in = [col_swap(y_parts[d], 0, d) for d in (2, 1, 3)]
    piece = z_here.shape[1:]
    shapes = [jax.ShapeDtypeStruct(piece, f32), jax.ShapeDtypeStruct(piece, bf16)]
    z_kept, z_send = small(merge_z_near, shapes, z_here, z_near)
    z_far = col_swap(z_send, 2, 0)
    features, z_kept = lax.optimization_barrier((features, z_kept))
    self_term = jnp.dot(features, self_weight, preferred_element_type=f32)
    self_term, z_far = lax.optimization_barrier((self_term, z_far))
    block = (FIRST + own.shape[1], width)
    shapes = [jax.ShapeDtypeStruct(block, f32)] * 2 + [jax.ShapeDtypeStruct((2, *block), bf16)]
    here, across, send = small(merge_z_far, shapes, z_kept, z_far, own)
    got = col_swap(send, 0, 1)
    y_in, across = lax.optimization_barrier((y_in, across))
    shapes = [jax.ShapeDtypeStruct(own.shape[1:], bf16)] * (Z - 1)
    y_send = list(small(merge_y, shapes, y_parts[0], *y_in))
    y_last = [col_swap(y_send[e - 1], e, 0) for e in (2, 3, 1)]
    y_send[0], got = lax.optimization_barrier((y_send[0], got))
    shapes = [jax.ShapeDtypeStruct(block, f32), jax.ShapeDtypeStruct(block, bf16)]
    here, send = small(merge_z_last, shapes, here, across, got)
    last = col_swap(send, 0, 3)
    y_sum = sum(part.astype(f32) for part in y_last)
    last, y_sum = lax.optimization_barrier((last, y_sum))
    here += last.astype(f32)
    return jnp.concatenate([here[:FIRST], here[FIRST:] + y_sum], axis=0), self_term


def per_device(
    features, self_weight, rel_weight, bias, blocks, block_rows, block_cols, block_counts
):
    relations, slots, size, _ = blocks.shape[2:]
    weights = jnp.transpose(rel_weight, (1, 0, 2))
    blocks = blocks.reshape(relations * slots, size, size)
    to_plan = (block_rows, block_cols, block_counts)
    parts = gather_groups(features, to_plan, blocks, weights)
    owned, self_term = scatter_sum(parts, features, self_weight)
    return jnp.maximum(self_term + owned + bias, 0.0).astype(jnp.bfloat16)


def solution(mesh):
    return jax.shard_map(
        per_device,
        mesh=mesh,
        in_specs=(
            P(("row", "col"), None),
            P(),
            P(),
            P(),
            P("row", "col", None, None, None, None),
            P("row", "col", None, None),
            P("row", "col", None, None),
            P("row", "col", None),
        ),
        out_specs=P(("row", "col"), None),
        check_vma=False,
    )
```

```python
import functools

import jax
import jax.numpy as jnp
from jax import lax
from jax.experimental import pallas as pl
from jax.experimental.pallas import tpu as pltpu
from jax.sharding import PartitionSpec as P

Z, Y = 4, 4
FIRST = 32
UNROLL, QUAD = 4, 4


def row_swap(value, dz, dx, dc):
    return lax.ppermute(value, "row", [(at, at ^ (dz * 8 + dx * 2 + dc)) for at in range(16)])


def col_swap(value, dz, dy):
    return lax.ppermute(value, "col", [(at, at ^ (dz * Y + dy)) for at in range(16)])


def rows_at(index, size):
    return pl.ds(pl.multiple_of(index * size, size), size)


def stage_kernel(group, first, last, codes_ref, starts_ref, blocks_ref, weight_ref, group_ref, *refs):
    if not first:
        refs = refs[1:]
    total, refs = refs[0], refs[1:]
    if last:
        y_refs, z_refs, own_ref, refs = refs[:Y], refs[Y : Y + 2], refs[Y + 2], refs[Y + 3 :]
    (picked,) = refs
    relations = weight_ref.shape[0]
    size = blocks_ref.shape[-1]
    if first:
        total[...] = jnp.zeros_like(total)
    base = starts_ref[group * relations]
    length = starts_ref[(group + 1) * relations] - base

    def pick(step, carry):
        for u in range(UNROLL):
            n = jnp.minimum(step * UNROLL + u, length - 1)
            code = codes_ref[base + n]
            product = jnp.dot(
                blocks_ref[code // 64],
                group_ref[rows_at(code // 16 % 4, size), :],
                preferred_element_type=jnp.float32,
            )
            picked[rows_at(n, size), :] = product.astype(picked.dtype)
        return carry

    lax.fori_loop(0, (length + UNROLL - 1) // UNROLL, pick, 0)

    def spread(relation, carry):
        start = starts_ref[group * relations + relation]
        end = starts_ref[group * relations + relation + 1]

        def quad(step, carry):
            begin = start + step * QUAD
            for count in range(1, QUAD + 1):
                enough = (end - begin >= count) if count == QUAD else (end - begin == count)

                @pl.when(enough)
                def _():
                    moved = jnp.dot(
                        picked[pl.ds(pl.multiple_of((begin - base) * size, size), count * size), :],
                        weight_ref[relation],
                        preferred_element_type=jnp.float32,
                    )
                    for part in range(count):
                        target = rows_at(codes_ref[begin + part] % 16, size)
                        total[target, :] += moved[part * size : (part + 1) * size]

            return carry

        return lax.fori_loop(0, (end - start + QUAD - 1) // QUAD, quad, carry)

    lax.fori_loop(0, relations, spread, 0)
    if last:
        for d in range(Y):
            for e in range(Z):
                rows = total[(d * Z + e) * size : (d * Z + e + 1) * size, :].astype(jnp.bfloat16)
                z_refs[e % 2][e // 2, d] = rows[:FIRST]
                if e == 0:
                    own_ref[d] = rows[FIRST:]
                else:
                    y_refs[d][e - 1] = rows[FIRST:]


def plan_kernel(table_ref, codes_ref, starts_ref):
    relations, slots = table_ref.shape
    row_me, col_me = lax.axis_index("row"), lax.axis_index("col")
    for index in range(4 * relations + 1):
        starts_ref[index] = 0

    def parts(relation, slot):
        packed = table_ref[relation, slot]
        source = (packed >> 4 & 15) ^ row_me
        target = (packed & 15) ^ col_me
        return packed >> 8, (source >> 3) * 2 + (source & 1), source >> 1 & 3, (target & 3) * 4 + (target >> 2)

    def per_slot(act):
        for relation in range(relations):
            live = table_ref[relation, 0] >> 8

            def body(slot, carry):
                at = relation * slots + slot
                _, group, place, target = parts(relation, slot)
                act(group * relations + relation, at, place, target)
                return carry

            lax.fori_loop(0, live, body, 0)

    def count(index, at, place, target):
        starts_ref[index + 1] = starts_ref[index + 1] + 1

    def put(index, at, place, target):
        spot = starts_ref[index]
        codes_ref[spot] = at * 64 + place * 16 + target
        starts_ref[index] = spot + 1

    per_slot(count)
    for index in range(1, 4 * relations + 1):
        starts_ref[index] = starts_ref[index] + starts_ref[index - 1]
    per_slot(put)
    for index in range(4 * relations - 1, 0, -1):
        starts_ref[index] = starts_ref[index - 1]
    starts_ref[0] = 0


def plan(block_rows, block_cols, block_counts):
    relations, slots = block_rows.shape[2:]
    smem = pl.BlockSpec(memory_space=pltpu.SMEM)
    many = relations * slots
    table = (block_rows + block_cols * 16 + block_counts[..., None] * 256)[0, 0]
    return pl.pallas_call(
        plan_kernel,
        out_shape=[
            jax.ShapeDtypeStruct((many,), jnp.int32),
            jax.ShapeDtypeStruct((4 * relations + 1,), jnp.int32),
        ],
        in_specs=[smem],
        out_specs=[smem] * 2,
        compiler_params=pltpu.CompilerParams(vmem_limit_bytes=1 << 20),
        name="plan",
    )(table)


def tile_stage(group, tables, blocks, weights, value, total):
    many, size, _ = blocks.shape
    width = weights.shape[-1]
    first, last = group == 0, group == 3
    vmem = pl.BlockSpec(memory_space=pltpu.VMEM)
    smem = pl.BlockSpec(memory_space=pltpu.SMEM)
    out_shape = [jax.ShapeDtypeStruct((Y * Z * size, width), jnp.float32)]
    if last:
        out_shape += [jax.ShapeDtypeStruct((Z - 1, size - FIRST, width), jnp.bfloat16)] * Y
        out_shape += [jax.ShapeDtypeStruct((Z // 2, Y, FIRST, width), jnp.bfloat16)] * 2
        out_shape += [jax.ShapeDtypeStruct((Y, size - FIRST, width), jnp.bfloat16)]
    args = [*tables, blocks, weights, value]
    if not first:
        args.append(total)
    return pl.pallas_call(
        functools.partial(stage_kernel, group, first, last),
        out_shape=out_shape,
        in_specs=[smem] * 2 + [vmem] * (len(args) - 2),
        out_specs=[vmem] * len(out_shape),
        scratch_shapes=[pltpu.VMEM((many * size, width), jnp.bfloat16)],
        input_output_aliases={} if first else {len(args) - 1: 0},
        compiler_params=pltpu.CompilerParams(vmem_limit_bytes=14 << 20),
        cost_estimate=pl.CostEstimate(flops=1 << 30, bytes_accessed=4 << 20, transcendentals=0),
        name="tile",
    )(*args)


def small(function, out_shape, *args):
    def kernel(*refs):
        function(refs[: len(args)], refs[len(args) :])

    vmem = pl.BlockSpec(memory_space=pltpu.VMEM)
    return pl.pallas_call(
        kernel,
        out_shape=out_shape,
        in_specs=[vmem] * len(args),
        out_specs=[vmem] * len(out_shape),
        compiler_params=pltpu.CompilerParams(vmem_limit_bytes=4 << 20),
        name="merge",
    )(*args)


def merge_y(ins, outs):
    for e in range(Z - 1):
        outs[e][...] = sum(ref[e].astype(jnp.float32) for ref in ins).astype(jnp.bfloat16)


def merge_z_near(ins, outs):
    own, got = ins
    outs[0][...] = own[0].astype(jnp.float32) + got[0].astype(jnp.float32)
    outs[1][...] = (own[1].astype(jnp.float32) + got[1].astype(jnp.float32)).astype(jnp.bfloat16)


def merge_z_far(ins, outs):
    kept, got, own = ins
    for d in range(Y):
        top = kept[d] + got[d].astype(jnp.float32)
        if d == 0 or d == 3:
            outs[d // 3][:FIRST, :] = top
            outs[d // 3][FIRST:, :] = own[d].astype(jnp.float32)
        else:
            outs[2][d - 1, :FIRST, :] = top.astype(jnp.bfloat16)
            outs[2][d - 1, FIRST:, :] = own[d]


def merge_z_last(ins, outs):
    here, across, got = ins
    outs[0][...] = here[...] + got[0].astype(jnp.float32)
    outs[1][...] = (across[...] + got[1].astype(jnp.float32)).astype(jnp.bfloat16)


def load_kernel(blocks_ref, weights_ref, blocks_out, weights_out):
    blocks_out[...] = blocks_ref[...]
    weights_out[...] = weights_ref[...]


def load(blocks, weights):
    vmem = pl.BlockSpec(memory_space=pltpu.VMEM)
    return pl.pallas_call(
        load_kernel,
        out_shape=[jax.ShapeDtypeStruct(a.shape, a.dtype) for a in (blocks, weights)],
        in_specs=[vmem] * 2,
        out_specs=[vmem] * 2,
        compiler_params=pltpu.CompilerParams(vmem_limit_bytes=2 << 20),
        name="load",
    )(blocks, weights)


def gather_groups(features, to_plan, blocks, weights):
    far = row_swap(features, 1, 0, 0)
    near_parts = [features] + [row_swap(features, 0, d, 0) for d in (1, 2, 3)]
    blocks, weights = load(blocks, weights)
    far, blocks, weights, to_plan = lax.optimization_barrier((far, blocks, weights, to_plan))
    tables = plan(*to_plan)
    stage = lambda index, value, total: tile_stage(index, tables, blocks, weights, value, total)
    far_parts = [far] + [row_swap(far, 0, d, 0) for d in (1, 2, 3)]
    near = jnp.concatenate(near_parts, axis=0)
    near_other = row_swap(near, 0, 0, 1)
    (total,) = stage(0, near, None)
    far_parts[-1], total = lax.optimization_barrier((far_parts[-1], total))
    rest = jnp.concatenate(far_parts, axis=0)
    rest_other = row_swap(rest, 0, 0, 1)
    (total,) = stage(1, near_other, total)
    (total,) = stage(2, rest, total)
    return stage(3, rest_other, total)[1:]


def scatter_sum(parts, features, self_weight):
    y_parts, (z_here, z_there, own) = parts[:Y], parts[Y:]
    f32, bf16 = jnp.float32, jnp.bfloat16
    width = own.shape[-1]
    z_near = col_swap(z_there, 1, 0)
    y_in = [col_swap(y_parts[d], 0, d) for d in (2, 1, 3)]
    piece = z_here.shape[1:]
    shapes = [jax.ShapeDtypeStruct(piece, f32), jax.ShapeDtypeStruct(piece, bf16)]
    z_kept, z_send = small(merge_z_near, shapes, z_here, z_near)
    z_far = col_swap(z_send, 2, 0)
    features, z_kept = lax.optimization_barrier((features, z_kept))
    self_term = jnp.dot(features, self_weight, preferred_element_type=f32)
    self_term, z_far = lax.optimization_barrier((self_term, z_far))
    block = (FIRST + own.shape[1], width)
    shapes = [jax.ShapeDtypeStruct(block, f32)] * 2 + [jax.ShapeDtypeStruct((2, *block), bf16)]
    here, across, send = small(merge_z_far, shapes, z_kept, z_far, own)
    got = col_swap(send, 0, 1)
    y_in, across = lax.optimization_barrier((y_in, across))
    shapes = [jax.ShapeDtypeStruct(own.shape[1:], bf16)] * (Z - 1)
    y_send = list(small(merge_y, shapes, y_parts[0], *y_in))
    y_last = [col_swap(y_send[e - 1], e, 0) for e in (2, 3, 1)]
    y_send[0], got = lax.optimization_barrier((y_send[0], got))
    shapes = [jax.ShapeDtypeStruct(block, f32), jax.ShapeDtypeStruct(block, bf16)]
    here, send = small(merge_z_last, shapes, here, across, got)
    last = col_swap(send, 0, 3)
    y_sum = sum(part.astype(f32) for part in y_last)
    last, y_sum = lax.optimization_barrier((last, y_sum))
    here += last.astype(f32)
    return jnp.concatenate([here[:FIRST], here[FIRST:] + y_sum], axis=0), self_term


def per_device(
    features, self_weight, rel_weight, bias, blocks, block_rows, block_cols, block_counts
):
    relations, slots, size, _ = blocks.shape[2:]
    weights = jnp.transpose(rel_weight, (1, 0, 2))
    blocks = blocks.reshape(relations * slots, size, size)
    to_plan = (block_rows, block_cols, block_counts)
    parts = gather_groups(features, to_plan, blocks, weights)
    owned, self_term = scatter_sum(parts, features, self_weight)
    return jnp.maximum(self_term + owned + bias, 0.0).astype(jnp.bfloat16)


def solution(mesh):
    return jax.shard_map(
        per_device,
        mesh=mesh,
        in_specs=(
            P(("row", "col"), None),
            P(),
            P(),
            P(),
            P("row", "col", None, None, None, None),
            P("row", "col", None, None),
            P("row", "col", None, None),
            P("row", "col", None),
        ),
        out_specs=P(("row", "col"), None),
        check_vma=False,
    )
```

```python
import functools

import jax
import jax.numpy as jnp
from jax import lax
from jax.experimental import pallas as pl
from jax.experimental.pallas import tpu as pltpu
from jax.sharding import PartitionSpec as P

Z, Y = 4, 4
FIRST = 32
UNROLL, QUAD = 4, 4


def row_swap(value, dz, dx, dc):
    return lax.ppermute(value, "row", [(at, at ^ (dz * 8 + dx * 2 + dc)) for at in range(16)])


def col_swap(value, dz, dy):
    return lax.ppermute(value, "col", [(at, at ^ (dz * Y + dy)) for at in range(16)])


def rows_at(index, size):
    return pl.ds(pl.multiple_of(index * size, size), size)


def stage_kernel(group, first, last, codes_ref, starts_ref, blocks_ref, weight_ref, group_ref, *refs):
    if not first:
        refs = refs[1:]
    total, refs = refs[0], refs[1:]
    if last:
        y_refs, z_refs, own_ref, refs = refs[:Y], refs[Y : Y + 2], refs[Y + 2], refs[Y + 3 :]
    (picked,) = refs
    relations = weight_ref.shape[0]
    size = blocks_ref.shape[-1]
    if first:
        total[...] = jnp.zeros_like(total)
    base = starts_ref[group * relations]
    length = starts_ref[(group + 1) * relations] - base

    def pick(step, carry):
        for u in range(UNROLL):
            n = jnp.minimum(step * UNROLL + u, length - 1)
            code = codes_ref[base + n]
            product = jnp.dot(
                blocks_ref[code // 64],
                group_ref[rows_at(code // 16 % 4, size), :],
                preferred_element_type=jnp.float32,
            )
            picked[rows_at(n, size), :] = product.astype(picked.dtype)
        return carry

    lax.fori_loop(0, (length + UNROLL - 1) // UNROLL, pick, 0)

    def spread(relation, carry):
        start = starts_ref[group * relations + relation]
        end = starts_ref[group * relations + relation + 1]

        def quad(step, carry):
            begin = start + step * QUAD
            for count in range(1, QUAD + 1):
                enough = (end - begin >= count) if count == QUAD else (end - begin == count)

                @pl.when(enough)
                def _():
                    moved = jnp.dot(
                        picked[pl.ds(pl.multiple_of((begin - base) * size, size), count * size), :],
                        weight_ref[relation],
                        preferred_element_type=jnp.float32,
                    )
                    for part in range(count):
                        target = rows_at(codes_ref[begin + part] % 16, size)
                        total[target, :] += moved[part * size : (part + 1) * size]

            return carry

        return lax.fori_loop(0, (end - start + QUAD - 1) // QUAD, quad, carry)

    lax.fori_loop(0, relations, spread, 0)
    if last:
        for d in range(Y):
            for e in range(Z):
                rows = total[(d * Z + e) * size : (d * Z + e + 1) * size, :].astype(jnp.bfloat16)
                z_refs[e % 2][e // 2, d] = rows[:FIRST]
                if e == 0:
                    own_ref[d] = rows[FIRST:]
                else:
                    y_refs[d][e - 1] = rows[FIRST:]


def plan_kernel(table_ref, codes_ref, starts_ref):
    relations, slots = table_ref.shape
    row_me, col_me = lax.axis_index("row"), lax.axis_index("col")
    for index in range(4 * relations + 1):
        starts_ref[index] = 0

    def parts(relation, slot):
        packed = table_ref[relation, slot]
        source = (packed >> 4 & 15) ^ row_me
        target = (packed & 15) ^ col_me
        return packed >> 8, (source >> 3) * 2 + (source & 1), source >> 1 & 3, (target & 3) * 4 + (target >> 2)

    def per_slot(act):
        for relation in range(relations):
            live = table_ref[relation, 0] >> 8

            def body(slot, carry):
                at = relation * slots + slot
                _, group, place, target = parts(relation, slot)
                act(group * relations + relation, at, place, target)
                return carry

            lax.fori_loop(0, live, body, 0)

    def count(index, at, place, target):
        starts_ref[index + 1] = starts_ref[index + 1] + 1

    def put(index, at, place, target):
        spot = starts_ref[index]
        codes_ref[spot] = at * 64 + place * 16 + target
        starts_ref[index] = spot + 1

    per_slot(count)
    for index in range(1, 4 * relations + 1):
        starts_ref[index] = starts_ref[index] + starts_ref[index - 1]
    per_slot(put)
    for index in range(4 * relations - 1, 0, -1):
        starts_ref[index] = starts_ref[index - 1]
    starts_ref[0] = 0


def plan(block_rows, block_cols, block_counts):
    relations, slots = block_rows.shape[2:]
    smem = pl.BlockSpec(memory_space=pltpu.SMEM)
    many = relations * slots
    table = (block_rows + block_cols * 16 + block_counts[..., None] * 256)[0, 0]
    return pl.pallas_call(
        plan_kernel,
        out_shape=[
            jax.ShapeDtypeStruct((many,), jnp.int32),
            jax.ShapeDtypeStruct((4 * relations + 1,), jnp.int32),
        ],
        in_specs=[smem],
        out_specs=[smem] * 2,
        compiler_params=pltpu.CompilerParams(vmem_limit_bytes=1 << 20),
        name="plan",
    )(table)


def tile_stage(group, tables, blocks, weights, value, total):
    many, size, _ = blocks.shape
    width = weights.shape[-1]
    first, last = group == 0, group == 3
    vmem = pl.BlockSpec(memory_space=pltpu.VMEM)
    smem = pl.BlockSpec(memory_space=pltpu.SMEM)
    out_shape = [jax.ShapeDtypeStruct((Y * Z * size, width), jnp.float32)]
    if last:
        out_shape += [jax.ShapeDtypeStruct((Z - 1, size - FIRST, width), jnp.bfloat16)] * Y
        out_shape += [jax.ShapeDtypeStruct((Z // 2, Y, FIRST, width), jnp.bfloat16)] * 2
        out_shape += [jax.ShapeDtypeStruct((Y, size - FIRST, width), jnp.bfloat16)]
    args = [*tables, blocks, weights, value]
    if not first:
        args.append(total)
    return pl.pallas_call(
        functools.partial(stage_kernel, group, first, last),
        out_shape=out_shape,
        in_specs=[smem] * 2 + [vmem] * (len(args) - 2),
        out_specs=[vmem] * len(out_shape),
        scratch_shapes=[pltpu.VMEM((many * size, width), jnp.bfloat16)],
        input_output_aliases={} if first else {len(args) - 1: 0},
        compiler_params=pltpu.CompilerParams(vmem_limit_bytes=14 << 20),
        cost_estimate=pl.CostEstimate(flops=1 << 30, bytes_accessed=4 << 20, transcendentals=0),
        name="tile",
    )(*args)


def small(function, out_shape, *args):
    def kernel(*refs):
        function(refs[: len(args)], refs[len(args) :])

    vmem = pl.BlockSpec(memory_space=pltpu.VMEM)
    return pl.pallas_call(
        kernel,
        out_shape=out_shape,
        in_specs=[vmem] * len(args),
        out_specs=[vmem] * len(out_shape),
        compiler_params=pltpu.CompilerParams(vmem_limit_bytes=4 << 20),
        name="merge",
    )(*args)


def merge_y(ins, outs):
    for e in range(Z - 1):
        outs[e][...] = sum(ref[e].astype(jnp.float32) for ref in ins).astype(jnp.bfloat16)


def merge_z_near(ins, outs):
    own, got = ins
    outs[0][...] = own[0].astype(jnp.float32) + got[0].astype(jnp.float32)
    outs[1][...] = (own[1].astype(jnp.float32) + got[1].astype(jnp.float32)).astype(jnp.bfloat16)


def merge_z_far(ins, outs):
    kept, got, own = ins
    for d in range(Y):
        top = kept[d] + got[d].astype(jnp.float32)
        if d == 0 or d == 3:
            outs[d // 3][:FIRST, :] = top
            outs[d // 3][FIRST:, :] = own[d].astype(jnp.float32)
        else:
            outs[2][d - 1, :FIRST, :] = top.astype(jnp.bfloat16)
            outs[2][d - 1, FIRST:, :] = own[d]


def merge_z_last(ins, outs):
    here, across, got = ins
    outs[0][...] = here[...] + got[0].astype(jnp.float32)
    outs[1][...] = (across[...] + got[1].astype(jnp.float32)).astype(jnp.bfloat16)


def load_kernel(blocks_ref, weights_ref, blocks_out, weights_out):
    blocks_out[...] = blocks_ref[...]
    weights_out[...] = weights_ref[...]


def load(blocks, weights):
    vmem = pl.BlockSpec(memory_space=pltpu.VMEM)
    return pl.pallas_call(
        load_kernel,
        out_shape=[jax.ShapeDtypeStruct(a.shape, a.dtype) for a in (blocks, weights)],
        in_specs=[vmem] * 2,
        out_specs=[vmem] * 2,
        compiler_params=pltpu.CompilerParams(vmem_limit_bytes=2 << 20),
        name="load",
    )(blocks, weights)


def gather_groups(features, to_plan, blocks, weights):
    far = row_swap(features, 1, 0, 0)
    near_parts = [features] + [row_swap(features, 0, d, 0) for d in (1, 2, 3)]
    blocks, weights = load(blocks, weights)
    far, blocks, weights, to_plan = lax.optimization_barrier((far, blocks, weights, to_plan))
    tables = plan(*to_plan)
    stage = lambda index, value, total: tile_stage(index, tables, blocks, weights, value, total)
    far_parts = [far] + [row_swap(far, 0, d, 0) for d in (1, 2, 3)]
    near = jnp.concatenate(near_parts, axis=0)
    near_other = row_swap(near, 0, 0, 1)
    (total,) = stage(0, near, None)
    (total,) = stage(1, near_other, total)
    far_parts[-1], total = lax.optimization_barrier((far_parts[-1], total))
    rest = jnp.concatenate(far_parts, axis=0)
    rest_other = row_swap(rest, 0, 0, 1)
    (total,) = stage(2, rest, total)
    return stage(3, rest_other, total)[1:]


def scatter_sum(parts, features, self_weight):
    y_parts, (z_here, z_there, own) = parts[:Y], parts[Y:]
    f32, bf16 = jnp.float32, jnp.bfloat16
    width = own.shape[-1]
    z_near = col_swap(z_there, 1, 0)
    y_in = [col_swap(y_parts[d], 0, d) for d in (1, 3, 2)]
    piece = z_here.shape[1:]
    shapes = [jax.ShapeDtypeStruct(piece, f32), jax.ShapeDtypeStruct(piece, bf16)]
    z_kept, z_send = small(merge_z_near, shapes, z_here, z_near)
    z_far = col_swap(z_send, 2, 0)
    features, z_kept = lax.optimization_barrier((features, z_kept))
    self_term = jnp.dot(features, self_weight, preferred_element_type=f32)
    self_term, z_far = lax.optimization_barrier((self_term, z_far))
    block = (FIRST + own.shape[1], width)
    shapes = [jax.ShapeDtypeStruct(block, f32)] * 2 + [jax.ShapeDtypeStruct((2, *block), bf16)]
    here, across, send = small(merge_z_far, shapes, z_kept, z_far, own)
    got = col_swap(send, 0, 1)
    y_in, across = lax.optimization_barrier((y_in, across))
    shapes = [jax.ShapeDtypeStruct(own.shape[1:], bf16)] * (Z - 1)
    y_send = list(small(merge_y, shapes, y_parts[0], *y_in))
    y_last = [col_swap(y_send[e - 1], e, 0) for e in (2, 3, 1)]
    y_send[0], got = lax.optimization_barrier((y_send[0], got))
    shapes = [jax.ShapeDtypeStruct(block, f32), jax.ShapeDtypeStruct(block, bf16)]
    here, send = small(merge_z_last, shapes, here, across, got)
    last = col_swap(send, 0, 3)
    y_sum = sum(part.astype(f32) for part in y_last)
    last, y_sum = lax.optimization_barrier((last, y_sum))
    here += last.astype(f32)
    return jnp.concatenate([here[:FIRST], here[FIRST:] + y_sum], axis=0), self_term


def per_device(
    features, self_weight, rel_weight, bias, blocks, block_rows, block_cols, block_counts
):
    relations, slots, size, _ = blocks.shape[2:]
    weights = jnp.transpose(rel_weight, (1, 0, 2))
    blocks = blocks.reshape(relations * slots, size, size)
    to_plan = (block_rows, block_cols, block_counts)
    parts = gather_groups(features, to_plan, blocks, weights)
    owned, self_term = scatter_sum(parts, features, self_weight)
    return jnp.maximum(self_term + owned + bias, 0.0).astype(jnp.bfloat16)


def solution(mesh):
    return jax.shard_map(
        per_device,
        mesh=mesh,
        in_specs=(
            P(("row", "col"), None),
            P(),
            P(),
            P(),
            P("row", "col", None, None, None, None),
            P("row", "col", None, None),
            P("row", "col", None, None),
            P("row", "col", None),
        ),
        out_specs=P(("row", "col"), None),
        check_vma=False,
    )
```

```python
import functools

import jax
import jax.numpy as jnp
from jax import lax
from jax.experimental import pallas as pl
from jax.experimental.pallas import tpu as pltpu
from jax.sharding import PartitionSpec as P

Z, Y = 4, 4
FIRST = 32
UNROLL, QUAD = 4, 4


def row_swap(value, dz, dx, dc):
    return lax.ppermute(value, "row", [(at, at ^ (dz * 8 + dx * 2 + dc)) for at in range(16)])


def col_swap(value, dz, dy):
    return lax.ppermute(value, "col", [(at, at ^ (dz * Y + dy)) for at in range(16)])


def rows_at(index, size):
    return pl.ds(pl.multiple_of(index * size, size), size)


def stage_kernel(group, first, last, codes_ref, starts_ref, blocks_ref, weight_ref, group_ref, *refs):
    if not first:
        refs = refs[1:]
    total, refs = refs[0], refs[1:]
    if last:
        y_refs, z_refs, own_ref, refs = refs[:Y], refs[Y : Y + 2], refs[Y + 2], refs[Y + 3 :]
    (picked,) = refs
    relations = weight_ref.shape[0]
    size = blocks_ref.shape[-1]
    if first:
        total[...] = jnp.zeros_like(total)
    base = starts_ref[group * relations]
    length = starts_ref[(group + 1) * relations] - base

    def pick(step, carry):
        for u in range(UNROLL):
            n = jnp.minimum(step * UNROLL + u, length - 1)
            code = codes_ref[base + n]
            product = jnp.dot(
                blocks_ref[code // 64],
                group_ref[rows_at(code // 16 % 4, size), :],
                preferred_element_type=jnp.float32,
            )
            picked[rows_at(n, size), :] = product.astype(picked.dtype)
        return carry

    lax.fori_loop(0, (length + UNROLL - 1) // UNROLL, pick, 0)

    def spread(relation, carry):
        start = starts_ref[group * relations + relation]
        end = starts_ref[group * relations + relation + 1]

        def quad(step, carry):
            begin = start + step * QUAD
            for count in range(1, QUAD + 1):
                enough = (end - begin >= count) if count == QUAD else (end - begin == count)

                @pl.when(enough)
                def _():
                    moved = jnp.dot(
                        picked[pl.ds(pl.multiple_of((begin - base) * size, size), count * size), :],
                        weight_ref[relation],
                        preferred_element_type=jnp.float32,
                    )
                    for part in range(count):
                        target = rows_at(codes_ref[begin + part] % 16, size)
                        total[target, :] += moved[part * size : (part + 1) * size]

            return carry

        return lax.fori_loop(0, (end - start + QUAD - 1) // QUAD, quad, carry)

    lax.fori_loop(0, relations, spread, 0)
    if last:
        for d in range(Y):
            for e in range(Z):
                rows = total[(d * Z + e) * size : (d * Z + e + 1) * size, :].astype(jnp.bfloat16)
                z_refs[e % 2][e // 2, d] = rows[:FIRST]
                if e == 0:
                    own_ref[d] = rows[FIRST:]
                else:
                    y_refs[d][e - 1] = rows[FIRST:]


def plan_kernel(table_ref, codes_ref, starts_ref):
    relations, slots = table_ref.shape
    row_me, col_me = lax.axis_index("row"), lax.axis_index("col")
    for index in range(4 * relations + 1):
        starts_ref[index] = 0

    def parts(relation, slot):
        packed = table_ref[relation, slot]
        source = (packed >> 4 & 15) ^ row_me
        target = (packed & 15) ^ col_me
        return packed >> 8, (source >> 3) * 2 + (source & 1), source >> 1 & 3, (target & 3) * 4 + (target >> 2)

    def per_slot(act):
        for relation in range(relations):
            live = table_ref[relation, 0] >> 8

            def body(slot, carry):
                at = relation * slots + slot
                _, group, place, target = parts(relation, slot)
                act(group * relations + relation, at, place, target)
                return carry

            lax.fori_loop(0, live, body, 0)

    def count(index, at, place, target):
        starts_ref[index + 1] = starts_ref[index + 1] + 1

    def put(index, at, place, target):
        spot = starts_ref[index]
        codes_ref[spot] = at * 64 + place * 16 + target
        starts_ref[index] = spot + 1

    per_slot(count)
    for index in range(1, 4 * relations + 1):
        starts_ref[index] = starts_ref[index] + starts_ref[index - 1]
    per_slot(put)
    for index in range(4 * relations - 1, 0, -1):
        starts_ref[index] = starts_ref[index - 1]
    starts_ref[0] = 0


def plan(block_rows, block_cols, block_counts):
    relations, slots = block_rows.shape[2:]
    smem = pl.BlockSpec(memory_space=pltpu.SMEM)
    many = relations * slots
    table = (block_rows + block_cols * 16 + block_counts[..., None] * 256)[0, 0]
    return pl.pallas_call(
        plan_kernel,
        out_shape=[
            jax.ShapeDtypeStruct((many,), jnp.int32),
            jax.ShapeDtypeStruct((4 * relations + 1,), jnp.int32),
        ],
        in_specs=[smem],
        out_specs=[smem] * 2,
        compiler_params=pltpu.CompilerParams(vmem_limit_bytes=1 << 20),
        name="plan",
    )(table)


def tile_stage(group, tables, blocks, weights, value, total):
    many, size, _ = blocks.shape
    width = weights.shape[-1]
    first, last = group == 0, group == 3
    vmem = pl.BlockSpec(memory_space=pltpu.VMEM)
    smem = pl.BlockSpec(memory_space=pltpu.SMEM)
    out_shape = [jax.ShapeDtypeStruct((Y * Z * size, width), jnp.float32)]
    if last:
        out_shape += [jax.ShapeDtypeStruct((Z - 1, size - FIRST, width), jnp.bfloat16)] * Y
        out_shape += [jax.ShapeDtypeStruct((Z // 2, Y, FIRST, width), jnp.bfloat16)] * 2
        out_shape += [jax.ShapeDtypeStruct((Y, size - FIRST, width), jnp.bfloat16)]
    args = [*tables, blocks, weights, value]
    if not first:
        args.append(total)
    return pl.pallas_call(
        functools.partial(stage_kernel, group, first, last),
        out_shape=out_shape,
        in_specs=[smem] * 2 + [vmem] * (len(args) - 2),
        out_specs=[vmem] * len(out_shape),
        scratch_shapes=[pltpu.VMEM((many * size, width), jnp.bfloat16)],
        input_output_aliases={} if first else {len(args) - 1: 0},
        compiler_params=pltpu.CompilerParams(vmem_limit_bytes=14 << 20),
        cost_estimate=pl.CostEstimate(flops=1 << 30, bytes_accessed=4 << 20, transcendentals=0),
        name="tile",
    )(*args)


def small(function, out_shape, *args):
    def kernel(*refs):
        function(refs[: len(args)], refs[len(args) :])

    vmem = pl.BlockSpec(memory_space=pltpu.VMEM)
    return pl.pallas_call(
        kernel,
        out_shape=out_shape,
        in_specs=[vmem] * len(args),
        out_specs=[vmem] * len(out_shape),
        compiler_params=pltpu.CompilerParams(vmem_limit_bytes=4 << 20),
        name="merge",
    )(*args)


def merge_y(ins, outs):
    for e in range(Z - 1):
        outs[e][...] = sum(ref[e].astype(jnp.float32) for ref in ins).astype(jnp.bfloat16)


def merge_z_near(ins, outs):
    own, got = ins
    outs[0][...] = own[0].astype(jnp.float32) + got[0].astype(jnp.float32)
    outs[1][...] = (own[1].astype(jnp.float32) + got[1].astype(jnp.float32)).astype(jnp.bfloat16)


def merge_z_far(ins, outs):
    kept, got, own = ins
    for d in range(Y):
        top = kept[d] + got[d].astype(jnp.float32)
        if d == 0 or d == 3:
            outs[d // 3][:FIRST, :] = top
            outs[d // 3][FIRST:, :] = own[d].astype(jnp.float32)
        else:
            outs[2][d - 1, :FIRST, :] = top.astype(jnp.bfloat16)
            outs[2][d - 1, FIRST:, :] = own[d]


def merge_z_last(ins, outs):
    here, across, got = ins
    outs[0][...] = here[...] + got[0].astype(jnp.float32)
    outs[1][...] = (across[...] + got[1].astype(jnp.float32)).astype(jnp.bfloat16)


def load_kernel(blocks_ref, weights_ref, blocks_out, weights_out):
    blocks_out[...] = blocks_ref[...]
    weights_out[...] = weights_ref[...]


def load(blocks, weights):
    vmem = pl.BlockSpec(memory_space=pltpu.VMEM)
    return pl.pallas_call(
        load_kernel,
        out_shape=[jax.ShapeDtypeStruct(a.shape, a.dtype) for a in (blocks, weights)],
        in_specs=[vmem] * 2,
        out_specs=[vmem] * 2,
        compiler_params=pltpu.CompilerParams(vmem_limit_bytes=2 << 20),
        name="load",
    )(blocks, weights)


def gather_groups(features, to_plan, blocks, weights):
    far = row_swap(features, 1, 0, 0)
    near_parts = [features] + [row_swap(features, 0, d, 0) for d in (1, 2, 3)]
    blocks, weights = load(blocks, weights)
    tables = plan(*to_plan)
    far, blocks, weights, tables = lax.optimization_barrier((far, blocks, weights, tables))
    near_parts[1], weights = lax.optimization_barrier((near_parts[1], weights))
    stage = lambda index, value, total: tile_stage(index, tables, blocks, weights, value, total)
    far_parts = [far] + [row_swap(far, 0, d, 0) for d in (1, 2, 3)]
    near = jnp.concatenate(near_parts, axis=0)
    near_other = row_swap(near, 0, 0, 1)
    (total,) = stage(0, near, None)
    (total,) = stage(1, near_other, total)
    far_parts[1:], total = lax.optimization_barrier((far_parts[1:], total))
    rest = jnp.concatenate(far_parts, axis=0)
    rest_other = row_swap(rest, 0, 0, 1)
    (total,) = stage(2, rest, total)
    return stage(3, rest_other, total)[1:]


def scatter_sum(parts, features, self_weight):
    y_parts, (z_here, z_there, own) = parts[:Y], parts[Y:]
    f32, bf16 = jnp.float32, jnp.bfloat16
    width = own.shape[-1]
    z_near = col_swap(z_there, 1, 0)
    y_in = [col_swap(y_parts[d], 0, d) for d in (2, 1, 3)]
    piece = z_here.shape[1:]
    shapes = [jax.ShapeDtypeStruct(piece, f32), jax.ShapeDtypeStruct(piece, bf16)]
    z_kept, z_send = small(merge_z_near, shapes, z_here, z_near)
    z_far = col_swap(z_send, 2, 0)
    features, z_kept = lax.optimization_barrier((features, z_kept))
    self_term = jnp.dot(features, self_weight, preferred_element_type=f32)
    self_term, z_far = lax.optimization_barrier((self_term, z_far))
    block = (FIRST + own.shape[1], width)
    shapes = [jax.ShapeDtypeStruct(block, f32)] * 2 + [jax.ShapeDtypeStruct((2, *block), bf16)]
    here, across, send = small(merge_z_far, shapes, z_kept, z_far, own)
    got = col_swap(send, 0, 1)
    y_in, across = lax.optimization_barrier((y_in, across))
    shapes = [jax.ShapeDtypeStruct(own.shape[1:], bf16)] * (Z - 1)
    y_send = list(small(merge_y, shapes, y_parts[0], *y_in))
    y_last = [col_swap(y_send[e - 1], e, 0) for e in (2, 3, 1)]
    y_send[0], got = lax.optimization_barrier((y_send[0], got))
    shapes = [jax.ShapeDtypeStruct(block, f32), jax.ShapeDtypeStruct(block, bf16)]
    here, send = small(merge_z_last, shapes, here, across, got)
    last = col_swap(send, 0, 3)
    y_sum = sum(part.astype(f32) for part in y_last)
    last, y_sum = lax.optimization_barrier((last, y_sum))
    here += last.astype(f32)
    return jnp.concatenate([here[:FIRST], here[FIRST:] + y_sum], axis=0), self_term


def per_device(
    features, self_weight, rel_weight, bias, blocks, block_rows, block_cols, block_counts
):
    relations, slots, size, _ = blocks.shape[2:]
    weights = jnp.transpose(rel_weight, (1, 0, 2))
    blocks = blocks.reshape(relations * slots, size, size)
    to_plan = (block_rows, block_cols, block_counts)
    parts = gather_groups(features, to_plan, blocks, weights)
    owned, self_term = scatter_sum(parts, features, self_weight)
    return jnp.maximum(self_term + owned + bias, 0.0).astype(jnp.bfloat16)


def solution(mesh):
    return jax.shard_map(
        per_device,
        mesh=mesh,
        in_specs=(
            P(("row", "col"), None),
            P(),
            P(),
            P(),
            P("row", "col", None, None, None, None),
            P("row", "col", None, None),
            P("row", "col", None, None),
            P("row", "col", None),
        ),
        out_specs=P(("row", "col"), None),
        check_vma=False,
    )
```

```python
import functools

import jax
import jax.numpy as jnp
from jax import lax
from jax.experimental import pallas as pl
from jax.experimental.pallas import tpu as pltpu
from jax.sharding import PartitionSpec as P

Z, Y = 4, 4
FIRST = 32
UNROLL, QUAD = 4, 4


def row_swap(value, dz, dx, dc):
    return lax.ppermute(value, "row", [(at, at ^ (dz * 8 + dx * 2 + dc)) for at in range(16)])


def col_swap(value, dz, dy):
    return lax.ppermute(value, "col", [(at, at ^ (dz * Y + dy)) for at in range(16)])


def rows_at(index, size):
    return pl.ds(pl.multiple_of(index * size, size), size)


def stage_kernel(group, last, codes_ref, starts_ref, blocks_ref, weight_ref, group_ref, *refs):
    refs = refs[1:]
    total, refs = refs[0], refs[1:]
    if last:
        y_refs, z_refs, own_ref, refs = refs[:Y], refs[Y : Y + 2], refs[Y + 2], refs[Y + 3 :]
    (picked,) = refs
    relations = weight_ref.shape[0]
    size = blocks_ref.shape[-1]
    base = starts_ref[group * relations]
    length = starts_ref[(group + 1) * relations] - base

    def pick(step, carry):
        for u in range(UNROLL):
            n = jnp.minimum(step * UNROLL + u, length - 1)
            code = codes_ref[base + n]
            product = jnp.dot(
                blocks_ref[code // 64],
                group_ref[rows_at(code // 16 % 4, size), :],
                preferred_element_type=jnp.float32,
            )
            picked[rows_at(n, size), :] = product.astype(picked.dtype)
        return carry

    lax.fori_loop(0, (length + UNROLL - 1) // UNROLL, pick, 0)

    def spread(relation, carry):
        start = starts_ref[group * relations + relation]
        end = starts_ref[group * relations + relation + 1]

        def quad(step, carry):
            begin = start + step * QUAD
            for count in range(1, QUAD + 1):
                enough = (end - begin >= count) if count == QUAD else (end - begin == count)

                @pl.when(enough)
                def _():
                    moved = jnp.dot(
                        picked[pl.ds(pl.multiple_of((begin - base) * size, size), count * size), :],
                        weight_ref[relation],
                        preferred_element_type=jnp.float32,
                    )
                    for part in range(count):
                        target = rows_at(codes_ref[begin + part] % 16, size)
                        total[target, :] += moved[part * size : (part + 1) * size]

            return carry

        return lax.fori_loop(0, (end - start + QUAD - 1) // QUAD, quad, carry)

    lax.fori_loop(0, relations, spread, 0)
    if last:
        for d in range(Y):
            for e in range(Z):
                rows = total[(d * Z + e) * size : (d * Z + e + 1) * size, :].astype(jnp.bfloat16)
                z_refs[e % 2][e // 2, d] = rows[:FIRST]
                if e == 0:
                    own_ref[d] = rows[FIRST:]
                else:
                    y_refs[d][e - 1] = rows[FIRST:]


def plan_kernel(table_ref, codes_ref, starts_ref):
    relations, slots = table_ref.shape
    row_me, col_me = lax.axis_index("row"), lax.axis_index("col")
    for index in range(4 * relations + 1):
        starts_ref[index] = 0

    def parts(relation, slot):
        packed = table_ref[relation, slot]
        source = (packed >> 4 & 15) ^ row_me
        target = (packed & 15) ^ col_me
        return packed >> 8, (source >> 3) * 2 + (source & 1), source >> 1 & 3, (target & 3) * 4 + (target >> 2)

    def per_slot(act):
        for relation in range(relations):
            live = table_ref[relation, 0] >> 8

            def body(slot, carry):
                at = relation * slots + slot
                _, group, place, target = parts(relation, slot)
                act(group * relations + relation, at, place, target)
                return carry

            lax.fori_loop(0, live, body, 0)

    def count(index, at, place, target):
        starts_ref[index + 1] = starts_ref[index + 1] + 1

    def put(index, at, place, target):
        spot = starts_ref[index]
        codes_ref[spot] = at * 64 + place * 16 + target
        starts_ref[index] = spot + 1

    per_slot(count)
    for index in range(1, 4 * relations + 1):
        starts_ref[index] = starts_ref[index] + starts_ref[index - 1]
    per_slot(put)
    for index in range(4 * relations - 1, 0, -1):
        starts_ref[index] = starts_ref[index - 1]
    starts_ref[0] = 0


def plan(block_rows, block_cols, block_counts):
    relations, slots = block_rows.shape[2:]
    smem = pl.BlockSpec(memory_space=pltpu.SMEM)
    many = relations * slots
    table = (block_rows + block_cols * 16 + block_counts[..., None] * 256)[0, 0]
    return pl.pallas_call(
        plan_kernel,
        out_shape=[
            jax.ShapeDtypeStruct((many,), jnp.int32),
            jax.ShapeDtypeStruct((4 * relations + 1,), jnp.int32),
        ],
        in_specs=[smem],
        out_specs=[smem] * 2,
        compiler_params=pltpu.CompilerParams(vmem_limit_bytes=1 << 20),
        name="plan",
    )(table)


def tile_stage(group, tables, blocks, weights, value, total):
    many, size, _ = blocks.shape
    width = weights.shape[-1]
    last = group == 3
    vmem = pl.BlockSpec(memory_space=pltpu.VMEM)
    smem = pl.BlockSpec(memory_space=pltpu.SMEM)
    out_shape = [jax.ShapeDtypeStruct((Y * Z * size, width), jnp.float32)]
    if last:
        out_shape += [jax.ShapeDtypeStruct((Z - 1, size - FIRST, width), jnp.bfloat16)] * Y
        out_shape += [jax.ShapeDtypeStruct((Z // 2, Y, FIRST, width), jnp.bfloat16)] * 2
        out_shape += [jax.ShapeDtypeStruct((Y, size - FIRST, width), jnp.bfloat16)]
    args = [*tables, blocks, weights, value]
    args.append(total)
    return pl.pallas_call(
        functools.partial(stage_kernel, group, last),
        out_shape=out_shape,
        in_specs=[smem] * 2 + [vmem] * (len(args) - 2),
        out_specs=[vmem] * len(out_shape),
        scratch_shapes=[pltpu.VMEM((many * size, width), jnp.bfloat16)],
        input_output_aliases={len(args) - 1: 0},
        compiler_params=pltpu.CompilerParams(vmem_limit_bytes=14 << 20),
        cost_estimate=pl.CostEstimate(flops=1 << 30, bytes_accessed=4 << 20, transcendentals=0),
        name="tile",
    )(*args)


def small(function, out_shape, *args):
    def kernel(*refs):
        function(refs[: len(args)], refs[len(args) :])

    vmem = pl.BlockSpec(memory_space=pltpu.VMEM)
    return pl.pallas_call(
        kernel,
        out_shape=out_shape,
        in_specs=[vmem] * len(args),
        out_specs=[vmem] * len(out_shape),
        compiler_params=pltpu.CompilerParams(vmem_limit_bytes=4 << 20),
        name="merge",
    )(*args)


def merge_y(ins, outs):
    for e in range(Z - 1):
        outs[e][...] = sum(ref[e].astype(jnp.float32) for ref in ins).astype(jnp.bfloat16)


def merge_z_near(ins, outs):
    own, got = ins
    outs[0][...] = own[0].astype(jnp.float32) + got[0].astype(jnp.float32)
    outs[1][...] = (own[1].astype(jnp.float32) + got[1].astype(jnp.float32)).astype(jnp.bfloat16)


def merge_z_far(ins, outs):
    kept, got, own = ins
    for d in range(Y):
        top = kept[d] + got[d].astype(jnp.float32)
        if d == 0 or d == 3:
            outs[d // 3][:FIRST, :] = top
            outs[d // 3][FIRST:, :] = own[d].astype(jnp.float32)
        else:
            outs[2][d - 1, :FIRST, :] = top.astype(jnp.bfloat16)
            outs[2][d - 1, FIRST:, :] = own[d]


def merge_z_last(ins, outs):
    here, across, got = ins
    outs[0][...] = here[...] + got[0].astype(jnp.float32)
    outs[1][...] = (across[...] + got[1].astype(jnp.float32)).astype(jnp.bfloat16)


def load_kernel(blocks_ref, weights_ref, blocks_out, weights_out, total):
    total[...] = jnp.zeros_like(total)
    blocks_out[...] = blocks_ref[...]
    weights_out[...] = weights_ref[...]


def load(blocks, weights):
    size, width = blocks.shape[-1], weights.shape[-1]
    vmem = pl.BlockSpec(memory_space=pltpu.VMEM)
    return pl.pallas_call(
        load_kernel,
        out_shape=[jax.ShapeDtypeStruct(a.shape, a.dtype) for a in (blocks, weights)]
        + [jax.ShapeDtypeStruct((Y * Z * size, width), jnp.float32)],
        in_specs=[vmem] * 2,
        out_specs=[vmem] * 3,
        compiler_params=pltpu.CompilerParams(vmem_limit_bytes=2 << 20),
        name="load",
    )(blocks, weights)


def gather_groups(features, to_plan, blocks, weights):
    far = row_swap(features, 1, 0, 0)
    near_parts = [features] + [row_swap(features, 0, d, 0) for d in (1, 2, 3)]
    blocks, weights, total = load(blocks, weights)
    far, blocks, weights, total, to_plan = lax.optimization_barrier((far, blocks, weights, total, to_plan))
    tables = plan(*to_plan)
    stage = lambda index, value, total: tile_stage(index, tables, blocks, weights, value, total)
    far_parts = [far] + [row_swap(far, 0, d, 0) for d in (1, 2, 3)]
    near = jnp.concatenate(near_parts, axis=0)
    near_other = row_swap(near, 0, 0, 1)
    (total,) = stage(0, near, total)
    (total,) = stage(1, near_other, total)
    far_parts[-1], total = lax.optimization_barrier((far_parts[-1], total))
    rest = jnp.concatenate(far_parts, axis=0)
    rest_other = row_swap(rest, 0, 0, 1)
    (total,) = stage(2, rest, total)
    return stage(3, rest_other, total)[1:]


def scatter_sum(parts, features, self_weight):
    y_parts, (z_here, z_there, own) = parts[:Y], parts[Y:]
    f32, bf16 = jnp.float32, jnp.bfloat16
    width = own.shape[-1]
    z_near = col_swap(z_there, 1, 0)
    y_in = [col_swap(y_parts[d], 0, d) for d in (2, 1, 3)]
    piece = z_here.shape[1:]
    shapes = [jax.ShapeDtypeStruct(piece, f32), jax.ShapeDtypeStruct(piece, bf16)]
    z_kept, z_send = small(merge_z_near, shapes, z_here, z_near)
    z_far = col_swap(z_send, 2, 0)
    features, z_kept = lax.optimization_barrier((features, z_kept))
    self_term = jnp.dot(features, self_weight, preferred_element_type=f32)
    self_term, z_far = lax.optimization_barrier((self_term, z_far))
    block = (FIRST + own.shape[1], width)
    shapes = [jax.ShapeDtypeStruct(block, f32)] * 2 + [jax.ShapeDtypeStruct((2, *block), bf16)]
    here, across, send = small(merge_z_far, shapes, z_kept, z_far, own)
    got = col_swap(send, 0, 1)
    y_in, across = lax.optimization_barrier((y_in, across))
    shapes = [jax.ShapeDtypeStruct(own.shape[1:], bf16)] * (Z - 1)
    y_send = list(small(merge_y, shapes, y_parts[0], *y_in))
    y_last = [col_swap(y_send[e - 1], e, 0) for e in (2, 3, 1)]
    y_send[0], got = lax.optimization_barrier((y_send[0], got))
    shapes = [jax.ShapeDtypeStruct(block, f32), jax.ShapeDtypeStruct(block, bf16)]
    here, send = small(merge_z_last, shapes, here, across, got)
    last = col_swap(send, 0, 3)
    y_sum = sum(part.astype(f32) for part in y_last)
    last, y_sum = lax.optimization_barrier((last, y_sum))
    here += last.astype(f32)
    return jnp.concatenate([here[:FIRST], here[FIRST:] + y_sum], axis=0), self_term


def per_device(
    features, self_weight, rel_weight, bias, blocks, block_rows, block_cols, block_counts
):
    relations, slots, size, _ = blocks.shape[2:]
    weights = jnp.transpose(rel_weight, (1, 0, 2))
    blocks = blocks.reshape(relations * slots, size, size)
    to_plan = (block_rows, block_cols, block_counts)
    parts = gather_groups(features, to_plan, blocks, weights)
    owned, self_term = scatter_sum(parts, features, self_weight)
    return jnp.maximum(self_term + owned + bias, 0.0).astype(jnp.bfloat16)


def solution(mesh):
    return jax.shard_map(
        per_device,
        mesh=mesh,
        in_specs=(
            P(("row", "col"), None),
            P(),
            P(),
            P(),
            P("row", "col", None, None, None, None),
            P("row", "col", None, None),
            P("row", "col", None, None),
            P("row", "col", None),
        ),
        out_specs=P(("row", "col"), None),
        check_vma=False,
    )
```

```python
import functools

import jax
import jax.numpy as jnp
from jax import lax
from jax.experimental import pallas as pl
from jax.experimental.pallas import tpu as pltpu
from jax.sharding import PartitionSpec as P

Z, Y = 4, 4
FIRST = 32
UNROLL, QUAD = 4, 4


def row_swap(value, dz, dx, dc):
    return lax.ppermute(value, "row", [(at, at ^ (dz * 8 + dx * 2 + dc)) for at in range(16)])


def col_swap(value, dz, dy):
    return lax.ppermute(value, "col", [(at, at ^ (dz * Y + dy)) for at in range(16)])


def rows_at(index, size):
    return pl.ds(pl.multiple_of(index * size, size), size)


def stage_kernel(group, last, codes_ref, starts_ref, blocks_ref, weight_ref, group_ref, *refs):
    refs = refs[1:]
    total, refs = refs[0], refs[1:]
    if last:
        y_refs, z_refs, own_ref, refs = refs[:Y], refs[Y : Y + 2], refs[Y + 2], refs[Y + 3 :]
    (picked,) = refs
    relations = weight_ref.shape[0]
    size = blocks_ref.shape[-1]
    base = starts_ref[group * relations]
    length = starts_ref[(group + 1) * relations] - base

    def pick(step, carry):
        for u in range(UNROLL):
            n = jnp.minimum(step * UNROLL + u, length - 1)
            code = codes_ref[base + n]
            product = jnp.dot(
                blocks_ref[code // 64],
                group_ref[rows_at(code // 16 % 4, size), :],
                preferred_element_type=jnp.float32,
            )
            picked[rows_at(n, size), :] = product.astype(picked.dtype)
        return carry

    lax.fori_loop(0, (length + UNROLL - 1) // UNROLL, pick, 0)

    def spread(relation, carry):
        start = starts_ref[group * relations + relation]
        end = starts_ref[group * relations + relation + 1]

        def quad(step, carry):
            begin = start + step * QUAD
            for count in range(1, QUAD + 1):
                enough = (end - begin >= count) if count == QUAD else (end - begin == count)

                @pl.when(enough)
                def _():
                    moved = jnp.dot(
                        picked[pl.ds(pl.multiple_of((begin - base) * size, size), count * size), :],
                        weight_ref[relation],
                        preferred_element_type=jnp.float32,
                    )
                    for part in range(count):
                        target = rows_at(codes_ref[begin + part] % 16, size)
                        total[target, :] += moved[part * size : (part + 1) * size]

            return carry

        return lax.fori_loop(0, (end - start + QUAD - 1) // QUAD, quad, carry)

    lax.fori_loop(0, relations, spread, 0)
    if last:
        for d in range(Y):
            for e in range(Z):
                rows = total[(d * Z + e) * size : (d * Z + e + 1) * size, :].astype(jnp.bfloat16)
                z_refs[e % 2][e // 2, d] = rows[:FIRST]
                if e == 0:
                    own_ref[d] = rows[FIRST:]
                else:
                    y_refs[d][e - 1] = rows[FIRST:]


def plan_kernel(table_ref, codes_ref, starts_ref):
    relations, slots = table_ref.shape
    row_me, col_me = lax.axis_index("row"), lax.axis_index("col")
    for index in range(4 * relations + 1):
        starts_ref[index] = 0

    def parts(relation, slot):
        packed = table_ref[relation, slot]
        source = (packed >> 4 & 15) ^ row_me
        target = (packed & 15) ^ col_me
        return packed >> 8, (source >> 3) * 2 + (source & 1), source >> 1 & 3, (target & 3) * 4 + (target >> 2)

    def per_slot(act):
        for relation in range(relations):
            live = table_ref[relation, 0] >> 8

            def body(slot, carry):
                at = relation * slots + slot
                _, group, place, target = parts(relation, slot)
                act(group * relations + relation, at, place, target)
                return carry

            lax.fori_loop(0, live, body, 0)

    def count(index, at, place, target):
        starts_ref[index + 1] = starts_ref[index + 1] + 1

    def put(index, at, place, target):
        spot = starts_ref[index]
        codes_ref[spot] = at * 64 + place * 16 + target
        starts_ref[index] = spot + 1

    per_slot(count)
    for index in range(1, 4 * relations + 1):
        starts_ref[index] = starts_ref[index] + starts_ref[index - 1]
    per_slot(put)
    for index in range(4 * relations - 1, 0, -1):
        starts_ref[index] = starts_ref[index - 1]
    starts_ref[0] = 0


def plan(block_rows, block_cols, block_counts):
    relations, slots = block_rows.shape[2:]
    smem = pl.BlockSpec(memory_space=pltpu.SMEM)
    many = relations * slots
    table = (block_rows + block_cols * 16 + block_counts[..., None] * 256)[0, 0]
    return pl.pallas_call(
        plan_kernel,
        out_shape=[
            jax.ShapeDtypeStruct((many,), jnp.int32),
            jax.ShapeDtypeStruct((4 * relations + 1,), jnp.int32),
        ],
        in_specs=[smem],
        out_specs=[smem] * 2,
        compiler_params=pltpu.CompilerParams(vmem_limit_bytes=1 << 20),
        name="plan",
    )(table)


def tile_stage(group, tables, blocks, weights, value, total):
    many, size, _ = blocks.shape
    width = weights.shape[-1]
    last = group == 3
    vmem = pl.BlockSpec(memory_space=pltpu.VMEM)
    smem = pl.BlockSpec(memory_space=pltpu.SMEM)
    out_shape = [jax.ShapeDtypeStruct((Y * Z * size, width), jnp.float32)]
    if last:
        out_shape += [jax.ShapeDtypeStruct((Z - 1, size - FIRST, width), jnp.bfloat16)] * Y
        out_shape += [jax.ShapeDtypeStruct((Z // 2, Y, FIRST, width), jnp.bfloat16)] * 2
        out_shape += [jax.ShapeDtypeStruct((Y, size - FIRST, width), jnp.bfloat16)]
    args = [*tables, blocks, weights, value]
    args.append(total)
    return pl.pallas_call(
        functools.partial(stage_kernel, group, last),
        out_shape=out_shape,
        in_specs=[smem] * 2 + [vmem] * (len(args) - 2),
        out_specs=[vmem] * len(out_shape),
        scratch_shapes=[pltpu.VMEM((many * size, width), jnp.bfloat16)],
        input_output_aliases={len(args) - 1: 0},
        compiler_params=pltpu.CompilerParams(vmem_limit_bytes=14 << 20),
        cost_estimate=pl.CostEstimate(flops=1 << 30, bytes_accessed=4 << 20, transcendentals=0),
        name="tile",
    )(*args)


def small(function, out_shape, *args):
    def kernel(*refs):
        function(refs[: len(args)], refs[len(args) :])

    vmem = pl.BlockSpec(memory_space=pltpu.VMEM)
    return pl.pallas_call(
        kernel,
        out_shape=out_shape,
        in_specs=[vmem] * len(args),
        out_specs=[vmem] * len(out_shape),
        compiler_params=pltpu.CompilerParams(vmem_limit_bytes=4 << 20),
        name="merge",
    )(*args)


def merge_y(ins, outs):
    for e in range(Z - 1):
        outs[e][...] = sum(ref[e].astype(jnp.float32) for ref in ins).astype(jnp.bfloat16)


def merge_z_near(ins, outs):
    own, got = ins
    outs[0][...] = own[0].astype(jnp.float32) + got[0].astype(jnp.float32)
    outs[1][...] = (own[1].astype(jnp.float32) + got[1].astype(jnp.float32)).astype(jnp.bfloat16)


def merge_z_far(ins, outs):
    kept, got, own = ins
    for d in range(Y):
        top = kept[d] + got[d].astype(jnp.float32)
        if d == 0 or d == 3:
            outs[d // 3][:FIRST, :] = top
            outs[d // 3][FIRST:, :] = own[d].astype(jnp.float32)
        else:
            outs[2][d - 1, :FIRST, :] = top.astype(jnp.bfloat16)
            outs[2][d - 1, FIRST:, :] = own[d]


def merge_z_last(ins, outs):
    here, across, got = ins
    outs[0][...] = here[...] + got[0].astype(jnp.float32)
    outs[1][...] = (across[...] + got[1].astype(jnp.float32)).astype(jnp.bfloat16)


def load_kernel(blocks_ref, weights_ref, blocks_out, weights_out, total):
    total[...] = jnp.zeros_like(total)
    blocks_out[...] = blocks_ref[...]
    weights_out[...] = weights_ref[...]


def load(blocks, weights):
    size, width = blocks.shape[-1], weights.shape[-1]
    vmem = pl.BlockSpec(memory_space=pltpu.VMEM)
    return pl.pallas_call(
        load_kernel,
        out_shape=[jax.ShapeDtypeStruct(a.shape, a.dtype) for a in (blocks, weights)]
        + [jax.ShapeDtypeStruct((Y * Z * size, width), jnp.float32)],
        in_specs=[vmem] * 2,
        out_specs=[vmem] * 3,
        compiler_params=pltpu.CompilerParams(vmem_limit_bytes=2 << 20),
        name="load",
    )(blocks, weights)


def gather_groups(features, to_plan, blocks, weights):
    far = row_swap(features, 1, 0, 0)
    near_parts = [features] + [row_swap(features, 0, d, 0) for d in (1, 2, 3)]
    blocks, weights, total = load(blocks, weights)
    far, blocks, weights, total, to_plan = lax.optimization_barrier((far, blocks, weights, total, to_plan))
    tables = plan(*to_plan)
    stage = lambda index, value, total: tile_stage(index, tables, blocks, weights, value, total)
    far_parts = [far] + [row_swap(far, 0, d, 0) for d in (1, 2, 3)]
    near = jnp.concatenate(near_parts, axis=0)
    near_other = row_swap(near, 0, 0, 1)
    (total,) = stage(0, near, total)
    far_parts[-1], total = lax.optimization_barrier((far_parts[-1], total))
    rest = jnp.concatenate(far_parts, axis=0)
    rest_other = row_swap(rest, 0, 0, 1)
    (total,) = stage(1, near_other, total)
    (total,) = stage(2, rest, total)
    return stage(3, rest_other, total)[1:]


def scatter_sum(parts, features, self_weight):
    y_parts, (z_here, z_there, own) = parts[:Y], parts[Y:]
    f32, bf16 = jnp.float32, jnp.bfloat16
    width = own.shape[-1]
    z_near = col_swap(z_there, 1, 0)
    y_in = [col_swap(y_parts[d], 0, d) for d in (2, 1, 3)]
    piece = z_here.shape[1:]
    shapes = [jax.ShapeDtypeStruct(piece, f32), jax.ShapeDtypeStruct(piece, bf16)]
    z_kept, z_send = small(merge_z_near, shapes, z_here, z_near)
    z_far = col_swap(z_send, 2, 0)
    features, z_kept = lax.optimization_barrier((features, z_kept))
    self_term = jnp.dot(features, self_weight, preferred_element_type=f32)
    self_term, z_far = lax.optimization_barrier((self_term, z_far))
    block = (FIRST + own.shape[1], width)
    shapes = [jax.ShapeDtypeStruct(block, f32)] * 2 + [jax.ShapeDtypeStruct((2, *block), bf16)]
    here, across, send = small(merge_z_far, shapes, z_kept, z_far, own)
    got = col_swap(send, 0, 1)
    y_in, across = lax.optimization_barrier((y_in, across))
    shapes = [jax.ShapeDtypeStruct(own.shape[1:], bf16)] * (Z - 1)
    y_send = list(small(merge_y, shapes, y_parts[0], *y_in))
    y_last = [col_swap(y_send[e - 1], e, 0) for e in (2, 3, 1)]
    y_send[0], got = lax.optimization_barrier((y_send[0], got))
    shapes = [jax.ShapeDtypeStruct(block, f32), jax.ShapeDtypeStruct(block, bf16)]
    here, send = small(merge_z_last, shapes, here, across, got)
    last = col_swap(send, 0, 3)
    y_sum = sum(part.astype(f32) for part in y_last)
    last, y_sum = lax.optimization_barrier((last, y_sum))
    here += last.astype(f32)
    return jnp.concatenate([here[:FIRST], here[FIRST:] + y_sum], axis=0), self_term


def per_device(
    features, self_weight, rel_weight, bias, blocks, block_rows, block_cols, block_counts
):
    relations, slots, size, _ = blocks.shape[2:]
    weights = jnp.transpose(rel_weight, (1, 0, 2))
    blocks = blocks.reshape(relations * slots, size, size)
    to_plan = (block_rows, block_cols, block_counts)
    parts = gather_groups(features, to_plan, blocks, weights)
    owned, self_term = scatter_sum(parts, features, self_weight)
    return jnp.maximum(self_term + owned + bias, 0.0).astype(jnp.bfloat16)


def solution(mesh):
    return jax.shard_map(
        per_device,
        mesh=mesh,
        in_specs=(
            P(("row", "col"), None),
            P(),
            P(),
            P(),
            P("row", "col", None, None, None, None),
            P("row", "col", None, None),
            P("row", "col", None, None),
            P("row", "col", None),
        ),
        out_specs=P(("row", "col"), None),
        check_vma=False,
    )
```

```python
import functools

import jax
import jax.numpy as jnp
from jax import lax
from jax.experimental import pallas as pl
from jax.experimental.pallas import tpu as pltpu
from jax.sharding import PartitionSpec as P

Z, Y = 4, 4
FIRST = 32
UNROLL, QUAD = 4, 4


def row_swap(value, dz, dx, dc):
    return lax.ppermute(value, "row", [(at, at ^ (dz * 8 + dx * 2 + dc)) for at in range(16)])


def col_swap(value, dz, dy):
    return lax.ppermute(value, "col", [(at, at ^ (dz * Y + dy)) for at in range(16)])


def rows_at(index, size):
    return pl.ds(pl.multiple_of(index * size, size), size)


def stage_kernel(group, first, last, codes_ref, starts_ref, blocks_ref, weight_ref, group_ref, *refs):
    if not first:
        refs = refs[1:]
    total, refs = refs[0], refs[1:]
    if last:
        y_refs, z_refs, own_ref, refs = refs[:Y], refs[Y : Y + 2], refs[Y + 2], refs[Y + 3 :]
    (picked,) = refs
    relations = weight_ref.shape[0]
    size = blocks_ref.shape[-1]
    if first:
        total[...] = jnp.zeros_like(total)
    base = starts_ref[group * relations]
    length = starts_ref[(group + 1) * relations] - base

    def pick(step, carry):
        for u in range(UNROLL):
            n = jnp.minimum(step * UNROLL + u, length - 1)
            code = codes_ref[base + n]
            product = jnp.dot(
                blocks_ref[code // 64],
                group_ref[rows_at(code // 16 % 4, size), :],
                preferred_element_type=jnp.float32,
            )
            picked[rows_at(n, size), :] = product.astype(picked.dtype)
        return carry

    lax.fori_loop(0, (length + UNROLL - 1) // UNROLL, pick, 0)

    def spread(relation, carry):
        start = starts_ref[group * relations + relation]
        end = starts_ref[group * relations + relation + 1]

        def quad(step, carry):
            begin = start + step * QUAD
            for count in range(1, QUAD + 1):
                enough = (end - begin >= count) if count == QUAD else (end - begin == count)

                @pl.when(enough)
                def _():
                    moved = jnp.dot(
                        picked[pl.ds(pl.multiple_of((begin - base) * size, size), count * size), :],
                        weight_ref[relation],
                        preferred_element_type=jnp.float32,
                    )
                    for part in range(count):
                        target = rows_at(codes_ref[begin + part] % 16, size)
                        total[target, :] += moved[part * size : (part + 1) * size]

            return carry

        return lax.fori_loop(0, (end - start + QUAD - 1) // QUAD, quad, carry)

    lax.fori_loop(0, relations, spread, 0)
    if last:
        for d in range(Y):
            for e in range(Z):
                rows = total[(d * Z + e) * size : (d * Z + e + 1) * size, :].astype(jnp.bfloat16)
                z_refs[e % 2][e // 2, d] = rows[:FIRST]
                if e == 0:
                    own_ref[d] = rows[FIRST:]
                else:
                    y_refs[d][e - 1] = rows[FIRST:]


def plan_kernel(table_ref, codes_ref, starts_ref):
    relations, slots = table_ref.shape
    row_me, col_me = lax.axis_index("row"), lax.axis_index("col")
    for index in range(4 * relations + 1):
        starts_ref[index] = 0

    def parts(relation, slot):
        packed = table_ref[relation, slot]
        source = (packed >> 4 & 15) ^ row_me
        target = (packed & 15) ^ col_me
        return packed >> 8, (source >> 3) * 2 + (source & 1), source >> 1 & 3, (target & 3) * 4 + (target >> 2)

    def per_slot(act):
        for relation in range(relations):
            live = table_ref[relation, 0] >> 8

            def body(slot, carry):
                at = relation * slots + slot
                _, group, place, target = parts(relation, slot)
                act(group * relations + relation, at, place, target)
                return carry

            lax.fori_loop(0, live, body, 0)

    def count(index, at, place, target):
        starts_ref[index + 1] = starts_ref[index + 1] + 1

    def put(index, at, place, target):
        spot = starts_ref[index]
        codes_ref[spot] = at * 64 + place * 16 + target
        starts_ref[index] = spot + 1

    per_slot(count)
    for index in range(1, 4 * relations + 1):
        starts_ref[index] = starts_ref[index] + starts_ref[index - 1]
    per_slot(put)
    for index in range(4 * relations - 1, 0, -1):
        starts_ref[index] = starts_ref[index - 1]
    starts_ref[0] = 0


def plan(block_rows, block_cols, block_counts):
    relations, slots = block_rows.shape[2:]
    smem = pl.BlockSpec(memory_space=pltpu.SMEM)
    many = relations * slots
    table = (block_rows + block_cols * 16 + block_counts[..., None] * 256)[0, 0]
    return pl.pallas_call(
        plan_kernel,
        out_shape=[
            jax.ShapeDtypeStruct((many,), jnp.int32),
            jax.ShapeDtypeStruct((4 * relations + 1,), jnp.int32),
        ],
        in_specs=[smem],
        out_specs=[smem] * 2,
        compiler_params=pltpu.CompilerParams(vmem_limit_bytes=1 << 20),
        name="plan",
    )(table)


def tile_stage(group, tables, blocks, weights, value, total):
    many, size, _ = blocks.shape
    width = weights.shape[-1]
    first, last = group == 0, group == 3
    vmem = pl.BlockSpec(memory_space=pltpu.VMEM)
    smem = pl.BlockSpec(memory_space=pltpu.SMEM)
    out_shape = [jax.ShapeDtypeStruct((Y * Z * size, width), jnp.float32)]
    if last:
        out_shape += [jax.ShapeDtypeStruct((Z - 1, size - FIRST, width), jnp.bfloat16)] * Y
        out_shape += [jax.ShapeDtypeStruct((Z // 2, Y, FIRST, width), jnp.bfloat16)] * 2
        out_shape += [jax.ShapeDtypeStruct((Y, size - FIRST, width), jnp.bfloat16)]
    args = [*tables, blocks, weights, value]
    if not first:
        args.append(total)
    return pl.pallas_call(
        functools.partial(stage_kernel, group, first, last),
        out_shape=out_shape,
        in_specs=[smem] * 2 + [vmem] * (len(args) - 2),
        out_specs=[vmem] * len(out_shape),
        scratch_shapes=[pltpu.VMEM((many * size, width), jnp.bfloat16)],
        input_output_aliases={} if first else {len(args) - 1: 0},
        compiler_params=pltpu.CompilerParams(vmem_limit_bytes=14 << 20),
        cost_estimate=pl.CostEstimate(flops=1 << 30, bytes_accessed=4 << 20, transcendentals=0),
        name="tile",
    )(*args)


def small(function, out_shape, *args):
    def kernel(*refs):
        function(refs[: len(args)], refs[len(args) :])

    vmem = pl.BlockSpec(memory_space=pltpu.VMEM)
    return pl.pallas_call(
        kernel,
        out_shape=out_shape,
        in_specs=[vmem] * len(args),
        out_specs=[vmem] * len(out_shape),
        compiler_params=pltpu.CompilerParams(vmem_limit_bytes=4 << 20),
        name="merge",
    )(*args)


def merge_y(ins, outs):
    for e in range(Z - 1):
        outs[e][...] = sum(ref[e].astype(jnp.float32) for ref in ins).astype(jnp.bfloat16)


def merge_z_near(ins, outs):
    own, got = ins
    outs[0][...] = own[0].astype(jnp.float32) + got[0].astype(jnp.float32)
    outs[1][...] = (own[1].astype(jnp.float32) + got[1].astype(jnp.float32)).astype(jnp.bfloat16)


def merge_z_far(ins, outs):
    kept, got, own = ins
    for d in range(Y):
        top = kept[d] + got[d].astype(jnp.float32)
        if d == 0 or d == 3:
            outs[d // 3][:FIRST, :] = top
            outs[d // 3][FIRST:, :] = own[d].astype(jnp.float32)
        else:
            outs[2][d - 1, :FIRST, :] = top.astype(jnp.bfloat16)
            outs[2][d - 1, FIRST:, :] = own[d]


def merge_z_last(ins, outs):
    here, across, got = ins
    outs[0][...] = here[...] + got[0].astype(jnp.float32)
    outs[1][...] = (across[...] + got[1].astype(jnp.float32)).astype(jnp.bfloat16)


def load_kernel(blocks_ref, weights_ref, blocks_out, weights_out):
    blocks_out[...] = blocks_ref[...]
    weights_out[...] = weights_ref[...]


def load(blocks, weights):
    vmem = pl.BlockSpec(memory_space=pltpu.VMEM)
    return pl.pallas_call(
        load_kernel,
        out_shape=[jax.ShapeDtypeStruct(a.shape, a.dtype) for a in (blocks, weights)],
        in_specs=[vmem] * 2,
        out_specs=[vmem] * 2,
        compiler_params=pltpu.CompilerParams(vmem_limit_bytes=2 << 20),
        name="load",
    )(blocks, weights)


def gather_groups(features, to_plan, blocks, weights):
    far = row_swap(features, 1, 0, 0)
    near_parts = [features] + [row_swap(features, 0, d, 0) for d in (1, 2, 3)]
    blocks, weights = load(blocks, weights)
    far, blocks, weights, to_plan = lax.optimization_barrier((far, blocks, weights, to_plan))
    tables = plan(*to_plan)
    stage = lambda index, value, total: tile_stage(index, tables, blocks, weights, value, total)
    far_parts = [far] + [row_swap(far, 0, d, 0) for d in (1, 2, 3)]
    near = jnp.concatenate(near_parts, axis=0)
    near_other = row_swap(near, 0, 0, 1)
    (total,) = stage(0, near, None)
    (total,) = stage(1, near_other, total)
    far_parts[-1], total = lax.optimization_barrier((far_parts[-1], total))
    rest = jnp.concatenate(far_parts, axis=0)
    rest_other = row_swap(rest, 0, 0, 1)
    (total,) = stage(2, rest, total)
    return stage(3, rest_other, total)[1:]


def scatter_sum(parts, features, self_weight):
    y_parts, (z_here, z_there, own) = parts[:Y], parts[Y:]
    f32, bf16 = jnp.float32, jnp.bfloat16
    width = own.shape[-1]
    z_near = col_swap(z_there, 1, 0)
    y_in = [col_swap(y_parts[d], 0, d) for d in (2, 1, 3)]
    piece = z_here.shape[1:]
    shapes = [jax.ShapeDtypeStruct(piece, f32), jax.ShapeDtypeStruct(piece, bf16)]
    z_kept, z_send = small(merge_z_near, shapes, z_here, z_near)
    z_far = col_swap(z_send, 2, 0)
    features, z_kept = lax.optimization_barrier((features, z_kept))
    self_term = jnp.dot(features, self_weight, preferred_element_type=f32)
    self_term, z_far = lax.optimization_barrier((self_term, z_far))
    block = (FIRST + own.shape[1], width)
    shapes = [jax.ShapeDtypeStruct(block, f32)] * 2 + [jax.ShapeDtypeStruct((2, *block), bf16)]
    here, across, send = small(merge_z_far, shapes, z_kept, z_far, own)
    got = col_swap(send, 0, 1)
    y_in, across = lax.optimization_barrier((y_in, across))
    shapes = [jax.ShapeDtypeStruct(own.shape[1:], bf16)] * (Z - 1)
    y_send = list(small(merge_y, shapes, y_parts[0], *y_in))
    y_last = [col_swap(y_send[e - 1], e, 0) for e in (1, 2, 3)]
    y_send[0], got = lax.optimization_barrier((y_send[0], got))
    shapes = [jax.ShapeDtypeStruct(block, f32), jax.ShapeDtypeStruct(block, bf16)]
    here, send = small(merge_z_last, shapes, here, across, got)
    last = col_swap(send, 0, 3)
    y_sum = sum(part.astype(f32) for part in y_last)
    last, y_sum = lax.optimization_barrier((last, y_sum))
    here += last.astype(f32)
    return jnp.concatenate([here[:FIRST], here[FIRST:] + y_sum], axis=0), self_term


def per_device(
    features, self_weight, rel_weight, bias, blocks, block_rows, block_cols, block_counts
):
    relations, slots, size, _ = blocks.shape[2:]
    weights = jnp.transpose(rel_weight, (1, 0, 2))
    blocks = blocks.reshape(relations * slots, size, size)
    to_plan = (block_rows, block_cols, block_counts)
    parts = gather_groups(features, to_plan, blocks, weights)
    owned, self_term = scatter_sum(parts, features, self_weight)
    return jnp.maximum(self_term + owned + bias, 0.0).astype(jnp.bfloat16)


def solution(mesh):
    return jax.shard_map(
        per_device,
        mesh=mesh,
        in_specs=(
            P(("row", "col"), None),
            P(),
            P(),
            P(),
            P("row", "col", None, None, None, None),
            P("row", "col", None, None),
            P("row", "col", None, None),
            P("row", "col", None),
        ),
        out_specs=P(("row", "col"), None),
        check_vma=False,
    )
```
